32 devices in a mesh: event: 2 (over y), mesh: 16 (over z, x, core).
Axes of the slice: x: 2, y: 2, z: 4, core: 2. Of those that a mesh axis runs over, the one named last changes fastest.
Arguments:
- forward_before: float32 [2, 3, 128, 8, 128], P('event', None, 'mesh'), may hold values from -3 to 3
- forward_now: float32 [2, 3, 128, 8, 128], P('event', None, 'mesh'), may hold values from -3 to 3
- adjoint_after: float32 [2, 3, 128, 8, 128], P('event', None, 'mesh'), may hold values from -3 to 3
- adjoint_now: float32 [2, 3, 128, 8, 128], P('event', None, 'mesh'), may hold values from -3 to 3
- mass_density: float32 [125, 2048], P(None, 'mesh'), may hold values from 0.8 to 1.5
- lame_lambda: float32 [125, 2048], P(None, 'mesh'), may hold values from 0.3 to 1
- lame_mu: float32 [125, 2048], P(None, 'mesh'), may hold values from 0.3 to 1
- source_element: int32 [2], P('event'), may hold values from 0 to 2047
- source_offset: int32 [2, 3], P('event'), may hold values from 0 to 4
- source_force: float32 [2, 3, 3], P('event'), may hold values from -120 to 120
- receiver_element: int32 [2, 32], P('event'), may hold values from 0 to 2047
- receiver_offset: int32 [2, 32, 3], P('event'), may hold values from 0 to 4
- receiver_data: float32 [2, 3, 32, 3], P('event'), may hold values from -3 to 3
Outputs:
- forward_final: float32 [2, 3, 128, 8, 128], P('event', None, 'mesh')
- adjoint_final: float32 [2, 3, 128, 8, 128], P('event', None, 'mesh')
- kernels: float32 [2, 125, 2048], P(None, None, ('mesh', 'event'))
The draws below stay inside these ranges and needn't reach their ends.
Inputs may be any that keep to these rules, and one draw needn't show every extreme that they name: `source_element`: element e lies at depth layer e // 64, row (e // 32) % 2, column e % 32. `source_offset`: offsets along depth, row, column; a point on the fixed bottom plane takes no force. `receiver_element`: element e lies at depth layer e // 64, row (e // 32) % 2, column e % 32; receivers may share points. `receiver_offset`: offsets along depth, row, column; a receiver on the fixed bottom plane records zero and takes no force.
All inputs are finite; a program needn't handle non-finite values.
Results may differ from the reference program's by a relative error of at most 0.0003.
Values sent between devices are 32-bit elements; how exact they have to be, the bound alone decides.
A program may use at most 192 MiB of HBM per device.

```python
import math
import jax
import jax.numpy as jnp
import numpy as np
from jax import lax

EX = 32
EY = 2
EZ = 2
STEPS = 3
NREC = 32
NX = 128
NY = 8
NZ = 128
NEL = 2048
N_EVENT = 2
N_MESH = 16


def set_ends(values, rng, least, top_value):
    dims = values.shape
    spot = [jax.random.randint(jax.random.fold_in(rng, axis), (), 0, dims[axis]) for axis in range(len(dims))]
    values = values.at[tuple(spot)].set(least)
    longest = dims.index(max(dims))
    spot[longest] = (spot[longest] + 1) % dims[longest]
    return values.at[tuple(spot)].set(top_value)


def levels(rng, dims, cuts, least, top_value):
    loudness, own = 1.0, jax.random.fold_in(rng, 6)
    for position, blocks in cuts:
        draws = jnp.exp(jax.random.uniform(jax.random.fold_in(own, position), (blocks,), jnp.float32, least / len(cuts), top_value / len(cuts)))
        loudness = loudness * jnp.repeat(draws, dims[position] // blocks).reshape([-1 if axis == position else 1 for axis in range(len(dims))])
    return loudness


def normal_values(stream_key, shape, scale, bound, shards=(), held_as=jnp.bfloat16):
    loudness = levels(stream_key, shape, shards, -0.22, 0.18) if shards else 1.0
    result = jax.random.normal(stream_key, shape, jnp.float32) * scale * loudness
    return jnp.minimum(jnp.maximum(result, -bound), bound).astype(held_as)


def setup_inputs(seed: int = 0) -> dict:
    arg_keys = jax.random.split(jax.random.key(seed), 14)
    return {
        "forward_before": normal_values(arg_keys[0], (N_EVENT, 3, NZ, NY, NX), 0.5, 3.0, ((0, 2), (2, 16)), jnp.float32),
        "forward_now": normal_values(arg_keys[1], (N_EVENT, 3, NZ, NY, NX), 0.5, 3.0, ((0, 2), (2, 16)), jnp.float32),
        "adjoint_after": normal_values(arg_keys[2], (N_EVENT, 3, NZ, NY, NX), 0.5, 3.0, ((0, 2), (2, 16)), jnp.float32),
        "adjoint_now": normal_values(arg_keys[3], (N_EVENT, 3, NZ, NY, NX), 0.5, 3.0, ((0, 2), (2, 16)), jnp.float32),
        "mass_density": jnp.clip(jnp.exp(math.log(1.5) - 0.62860864 * jax.random.uniform(arg_keys[4], (125, NEL), jnp.float32) ** levels(arg_keys[4], (125, NEL), ((1, 16),), -0.2, 0.2)), 0.8, 1.5),
        "lame_lambda": jnp.clip(jnp.exp(math.log(1.0) - 1.2039728 * jax.random.uniform(arg_keys[5], (125, NEL), jnp.float32) ** levels(arg_keys[5], (125, NEL), ((1, 16),), -0.2, 0.2)), 0.3, 1.0),
        "lame_mu": jnp.clip(jnp.exp(math.log(1.0) - 1.2039728 * jax.random.uniform(arg_keys[6], (125, NEL), jnp.float32) ** levels(arg_keys[6], (125, NEL), ((1, 16),), -0.2, 0.2)), 0.3, 1.0),
        "source_element": jax.random.randint(arg_keys[7], (N_EVENT,), 0, NEL).astype(jnp.int32),
        "source_offset": set_ends(jax.random.randint(arg_keys[8], (N_EVENT, 3), 0, 5), jax.random.fold_in(arg_keys[8], 1), 0, 4).astype(jnp.int32),
        "source_force": normal_values(arg_keys[9], (N_EVENT, STEPS, 3), 20.0, 120.0, ((0, 2),), jnp.float32),
        "receiver_element": set_ends(jax.random.randint(arg_keys[10], (N_EVENT, NREC), 0, NEL), jax.random.fold_in(arg_keys[10], 1), 0, NEL - 1).astype(jnp.int32),
        "receiver_offset": set_ends(jax.random.randint(arg_keys[11], (N_EVENT, NREC, 3), 0, 5), jax.random.fold_in(arg_keys[11], 1), 0, 4).astype(jnp.int32),
        "receiver_data": normal_values(arg_keys[12], (N_EVENT, STEPS, NREC, 3), 0.5, 3.0, ((0, 2),), jnp.float32),
    }


time_step = 0.04
adjoint_gain = 25.0

def numpy_tables():
    gll_points = np.array([-1.0, -math.sqrt(3.0 / 7.0), 0.0, math.sqrt(3.0 / 7.0), 1.0])
    legendre = (35.0 * gll_points ** 4 - 30.0 * gll_points ** 2 + 3.0) / 8.0
    deriv_table = np.zeros((5, 5))
    for row_q in range(5):
        for col_k in range(5):
            if row_q != col_k:
                deriv_table[row_q, col_k] = legendre[row_q] / (legendre[col_k] * (gll_points[row_q] - gll_points[col_k]))
    deriv_table[0, 0] = -5.0
    deriv_table[4, 4] = 5.0
    gll_weights = np.array([0.1, 49.0 / 90.0, 32.0 / 45.0, 49.0 / 90.0, 0.1])
    cube_weights = gll_weights[:, None, None] * gll_weights[None, :, None] * gll_weights[None, None, :]
    return (deriv_table, cube_weights)

def gll_tables():
    deriv_table, cube_weights = numpy_tables()
    return (jnp.asarray(deriv_table, jnp.float32), jnp.asarray(cube_weights.reshape(5, 5, 5, 1), jnp.float32))

def five_point(values, axis_pos, flipped):
    deriv_np = numpy_tables()[0]
    slices = [lax.index_in_dim(values, k_pos, axis_pos, keepdims=True) for k_pos in range(5)]
    outputs = []
    for p_pos in range(5):
        total = None
        for k_pos in range(5):
            coef = float(deriv_np[k_pos, p_pos] if flipped else deriv_np[p_pos, k_pos])
            if coef == 0.0:
                continue
            term = coef * slices[k_pos]
            total = term if total is None else total + term
        outputs.append(total)
    return jnp.concatenate(outputs, axis=axis_pos)

def unfold_cycle(wave_field, axis_pos):
    shape_in = wave_field.shape
    blocks = shape_in[axis_pos] // 4
    blocked = wave_field.reshape(shape_in[:axis_pos] + (blocks, 4) + shape_in[axis_pos + 1:])
    following = jnp.roll(lax.slice_in_dim(blocked, 0, 1, axis=axis_pos + 1), -1, axis=axis_pos)
    return jnp.concatenate([blocked, following], axis=axis_pos + 1)

def fold_cycle(blocked, axis_pos):
    leading = lax.slice_in_dim(blocked, 0, 1, axis=axis_pos + 1) + jnp.roll(lax.slice_in_dim(blocked, 4, 5, axis=axis_pos + 1), 1, axis=axis_pos)
    merged = jnp.concatenate([leading, lax.slice_in_dim(blocked, 1, 4, axis=axis_pos + 1)], axis=axis_pos + 1)
    shape_mid = merged.shape
    return merged.reshape(shape_mid[:axis_pos] + (shape_mid[axis_pos] * 4,) + shape_mid[axis_pos + 2:])

def unfold_depth(wave_field):
    blocks = (wave_field.shape[1] - 1) // 4
    lower_part = wave_field[:, :4 * blocks].reshape((wave_field.shape[0], blocks, 4) + wave_field.shape[2:])
    upper_part = wave_field[:, 4::4][:, :, None]
    return jnp.concatenate([lower_part, upper_part], axis=2)

def fold_depth(blocked):
    upper_part = blocked[:, :, 4]
    carried = jnp.concatenate([jnp.zeros_like(upper_part[:, :1]), upper_part[:, :-1]], axis=1)
    leading = blocked[:, :, 0] + carried
    merged = jnp.concatenate([leading[:, :, None], blocked[:, :, 1:4]], axis=2)
    plane_vals = merged.reshape((blocked.shape[0], blocked.shape[1] * 4) + blocked.shape[3:])
    return jnp.concatenate([plane_vals, upper_part[:, -1:]], axis=1)

def to_local(extended):
    spread = unfold_depth(unfold_cycle(unfold_cycle(extended, 3), 2))
    channels = spread.shape[0]
    element_total = spread.shape[1] * spread.shape[3] * spread.shape[5]
    return spread.transpose(0, 2, 4, 6, 1, 3, 5).reshape(channels, 5, 5, 5, element_total)

def from_local(local_vals, depth_count, rows_y, cols_x):
    channels = local_vals.shape[0]
    blocked = local_vals.reshape(channels, 5, 5, 5, depth_count, rows_y, cols_x).transpose(0, 4, 1, 5, 2, 6, 3)
    return fold_cycle(fold_cycle(fold_depth(blocked), 2), 3)

def gradients(local_vals, deriv_table):
    along_z = five_point(local_vals, 1, False)
    along_y = five_point(local_vals, 2, False)
    along_x = five_point(local_vals, 3, False)
    return (along_x, along_y, along_z)

def stress_columns(grad_table, lam_local, mu_local):
    diverg = grad_table[0][0] + grad_table[1][1] + grad_table[2][2]
    columns = []
    for dir_j in range(3):
        components = []
        for comp_i in range(3):
            entry_value = mu_local * (grad_table[dir_j][comp_i] + grad_table[comp_i][dir_j])
            if comp_i == dir_j:
                entry_value = entry_value + lam_local * diverg
            components.append(entry_value)
        columns.append(jnp.stack(components))
    return columns

def internal_force(columns, deriv_table, cube_weights):
    force_x = five_point(columns[0] * cube_weights, 3, True)
    force_y = five_point(columns[1] * cube_weights, 2, True)
    force_z = five_point(columns[2] * cube_weights, 1, True)
    return force_x + force_y + force_z

def kernel_terms(grads_adj, grads_fwd, lam_local, mu_local):
    div_adj = grads_adj[0][0] + grads_adj[1][1] + grads_adj[2][2]
    div_fwd = grads_fwd[0][0] + grads_fwd[1][1] + grads_fwd[2][2]
    contraction = jnp.zeros_like(div_adj)
    for dir_j in range(3):
        for comp_i in range(3):
            strain_adj = 0.5 * (grads_adj[dir_j][comp_i] + grads_adj[comp_i][dir_j])
            strain_fwd = 0.5 * (grads_fwd[dir_j][comp_i] + grads_fwd[comp_i][dir_j])
            contraction = contraction + strain_adj * strain_fwd
    lam_term = -lam_local * div_adj * div_fwd
    mu_term = -2.0 * mu_local * contraction
    return jnp.stack([lam_term, mu_term]).reshape(2, 125, div_adj.shape[-1])

def point_index(element, offset, plane_start, planes, elems_y, elems_x):
    row_span = 4 * elems_y
    col_span = 4 * elems_x
    z_local = 4 * (element // (elems_y * elems_x)) + offset[..., 0] - plane_start
    y_pos = (4 * (element // elems_x % elems_y) + offset[..., 1]) % row_span
    x_pos = (4 * (element % elems_x) + offset[..., 2]) % col_span
    valid = (z_local >= 0) & (z_local < planes)
    flat_pos = (z_local * row_span + y_pos) * col_span + x_pos
    return jnp.where(valid, flat_pos, planes * row_span * col_span).astype(jnp.int32)

def evolve(previous, current, after, present, src_point, src_force, rec_points, rec_data, inverse_mass, lam_local, mu_local, extend_fn, assemble_fn, reduce_fn):
    deriv_table, cube_weights = gll_tables()
    point_total = current[0].size
    step_total = src_force.shape[0]

    def advance(ext_field, older_field, load_field):
        local_vals = to_local(ext_field)
        grad_parts = gradients(local_vals, deriv_table)
        force = assemble_fn(internal_force(stress_columns(grad_parts, lam_local, mu_local), deriv_table, cube_weights))
        wave_field = ext_field[:, :-1]
        return (2.0 * wave_field - older_field + time_step ** 2 * inverse_mass * (load_field - force), grad_parts)
    ext_now = extend_fn(current)
    stored = []
    residuals = []
    for moment in range(step_total):
        load_field = jnp.zeros((3, point_total), current.dtype).at[:, src_point].add(src_force[moment], mode='drop').reshape(current.shape)
        following, unused_grads = advance(ext_now, previous, load_field)
        record = jnp.take(following.reshape(3, point_total), rec_points, axis=1, mode='fill', fill_value=0.0)
        residuals.append(record.T - rec_data[moment])
        previous, current = (current, following)
        ext_now = extend_fn(current)
        stored.append(ext_now)
    kernel = None
    ext_adj = extend_fn(present)
    older_field = after
    for moment in reversed(range(step_total)):
        load_field = jnp.zeros((3, point_total), present.dtype).at[:, rec_points].add(adjoint_gain * residuals[moment].T, mode='drop').reshape(present.shape)
        following, grads_adj = advance(ext_adj, older_field, load_field)
        grads_fwd = gradients(to_local(stored[moment]), deriv_table)
        kernel_term = reduce_fn(time_step * kernel_terms(grads_adj, grads_fwd, lam_local, mu_local))
        kernel = kernel_term if kernel is None else kernel + kernel_term
        older_field = present
        present = following
        if moment > 0:
            ext_adj = extend_fn(present)
    return (current, present, kernel)

def reference(forward_before, forward_now, adjoint_after, adjoint_now, mass_density, lame_lambda, lame_mu, source_element, source_offset, source_force, receiver_element, receiver_offset, receiver_data):
    deriv_table, cube_weights = gll_tables()
    planes = 4 * EZ * N_MESH
    elem_count = EX * EY * EZ * N_MESH
    lam_local = lame_lambda.reshape(5, 5, 5, elem_count)
    mu_local = lame_mu.reshape(5, 5, 5, elem_count)

    def extend(wave_field):
        return jnp.concatenate([wave_field, jnp.zeros_like(wave_field[:, :1])], axis=1)

    def assemble(local_vals):
        return from_local(local_vals, planes // 4, EY, EX)[:, :-1]

    def keep_term(kernel_term):
        return kernel_term
    inverse_mass = 1.0 / assemble((cube_weights * mass_density.reshape(5, 5, 5, elem_count))[None])

    def one_event(kernel_sum, event_inputs):
        before_one, now_one, after_one, adj_one, src_elem_one, src_off_one, force_one, rec_elem_one, rec_off_one, data_one = event_inputs
        src_point = point_index(src_elem_one, src_off_one, 0, planes, EY, EX)
        rec_points = point_index(rec_elem_one, rec_off_one, 0, planes, EY, EX)
        final_forward, final_adjoint, kernel = evolve(before_one, now_one, after_one, adj_one, src_point, force_one, rec_points, data_one, inverse_mass, lam_local, mu_local, extend, assemble, keep_term)
        return (kernel_sum + kernel, (final_forward, final_adjoint))
    start_sum = jnp.zeros((2, 125, elem_count), jnp.float32)
    kernel_sum, finals = lax.scan(one_event, start_sum, (forward_before, forward_now, adjoint_after, adjoint_now, source_element, source_offset, source_force, receiver_element, receiver_offset, receiver_data))
    return (finals[0], finals[1], kernel_sum)
```

```python
import functools
import math

import jax
import jax.numpy as jnp
import numpy as np
from jax import lax
from jax.experimental import pallas as pl
from jax.experimental.pallas import tpu as pltpu
from jax.sharding import PartitionSpec as P

time_step = 0.04
adjoint_gain = 25.0
LANES = 128


def numpy_tables():
    gll_points = np.array([-1.0, -math.sqrt(3.0 / 7.0), 0.0, math.sqrt(3.0 / 7.0), 1.0])
    legendre = (35.0 * gll_points**4 - 30.0 * gll_points**2 + 3.0) / 8.0
    deriv_table = np.zeros((5, 5))
    for row_q in range(5):
        for col_k in range(5):
            if row_q != col_k:
                deriv_table[row_q, col_k] = legendre[row_q] / (
                    legendre[col_k] * (gll_points[row_q] - gll_points[col_k])
                )
    deriv_table[0, 0] = -5.0
    deriv_table[4, 4] = 5.0
    gll_weights = np.array([0.1, 49.0 / 90.0, 32.0 / 45.0, 49.0 / 90.0, 0.1])
    return (deriv_table, gll_weights)


DERIV, WEIGHTS = numpy_tables()


def constants():
    spread = np.zeros((4, LANES, 4, 4, 32), np.float32)
    for j in range(4):
        for ex in range(32):
            for c in range(4):
                spread[j, 4 * ex + c, c, j, ex] = 1.0
    spread = spread.reshape(512, 512)
    rows = np.zeros((5, 5, 8, 125), np.float32)
    cube = np.zeros((5, 5, 8, LANES), np.float32)
    for a in range(5):
        for b in range(5):
            for c in range(5):
                rows[a, c, b, (a * 5 + b) * 5 + c] = 1.0
                cube[a, c, b, :] = WEIGHTS[a] * WEIGHTS[b] * WEIGHTS[c]
    rows = rows.reshape(200, 125)
    dy = np.zeros((2, 5, 8, LANES), np.float32)
    for k in range(5):
        for b in range(5):
            dy[0, k, b, :] = DERIV[b, k]
            dy[1, k, b, :] = DERIV[k, b]
    dz = np.stack([DERIV, DERIV.T]).reshape(-1).astype(np.float32)
    bf = jnp.bfloat16
    return (
        jnp.asarray(spread, bf),
        jnp.asarray(np.ascontiguousarray(spread.T), bf),
        jnp.asarray(rows, bf),
        jnp.asarray(np.ascontiguousarray(rows.T), bf),
        jnp.asarray(cube),
        jnp.asarray(dy),
        jnp.asarray(dz),
    )


def split3(value):
    high = value.astype(jnp.bfloat16)
    rest = value - high.astype(jnp.float32)
    middle = rest.astype(jnp.bfloat16)
    low = (rest - middle.astype(jnp.float32)).astype(jnp.bfloat16)
    return (high, middle, low)


def dot(left, right):
    return jnp.dot(left, right, preferred_element_type=jnp.float32)


def move_right(values, table):
    high, middle, low = split3(values)
    return dot(high, table) + dot(middle, table) + dot(low, table)


def move_left(table, values):
    high, middle, low = split3(values)
    return dot(table, high) + dot(table, middle) + dot(table, low)


def roll_lane(value, shift):
    return pltpu.roll(value, shift % LANES, value.ndim - 1)


def lane_iota(ndim):
    return lax.broadcasted_iota(jnp.int32, (1,) * (ndim - 1) + (LANES,), ndim - 1)


def sub_iota(ndim):
    return lax.broadcasted_iota(jnp.int32, (1,) * (ndim - 2) + (8, LANES), ndim - 2)


def pick(mask, first, second):
    return jnp.where(jnp.broadcast_to(mask, first.shape), first, second)


def from_left(value):
    at_edge = lane_iota(value.ndim) % 32 == 0
    return pick(at_edge, roll_lane(value, -31), roll_lane(value, 1))


def from_right(value):
    at_edge = lane_iota(value.ndim) % 32 == 31
    return pick(at_edge, roll_lane(value, 31), roll_lane(value, -1))


def roll_sub(value):
    return pltpu.roll(value, 4, value.ndim - 2)


def assemble_xy(value):
    first = value[:, 0:1] + from_left(value[:, 4:5])
    value = jnp.concatenate([first, value[:, 1:4], from_right(first)], axis=1)
    swapped = roll_sub(value)
    other = pick(
        lane_iota(4) % 64 < 32, roll_lane(swapped, -32), roll_lane(swapped, 32)
    )
    return value + pick(sub_iota(4) % 4 == 0, other, jnp.zeros_like(other))


def kernel(
    n_mesh,
    n_event,
    steps,
    now_ref,
    before_ref,
    adj_ref,
    after_ref,
    rho_ref,
    lam_ref,
    mu_ref,
    src_ref,
    force_ref,
    rec_elem_ref,
    rec_off_ref,
    data_ref,
    spread_ref,
    gather_ref,
    rows_ref,
    rows_t_ref,
    cube_ref,
    dy_ref,
    dz_ref,
    final_f_ref,
    final_a_ref,
    out_ref,
    fields,
    stress,
    force,
    strains,
    ksum,
    clam,
    cmu,
    minv,
    halo_s,
    halo_r,
    up_s,
    up_r,
    down_s,
    down_r,
    ev_s,
    ev_r,
    s_up,
    r_up,
    s_down,
    r_down,
    s_ev,
    r_ev,
):
    me = lax.axis_index("mesh")
    event = lax.axis_index("event")
    has_up = me > 0
    has_down = me < n_mesh - 1

    barrier = pltpu.get_barrier_semaphore()

    @pl.when(has_up)
    def _():
        pl.semaphore_signal(barrier, inc=1, device_id={"mesh": me - 1})

    @pl.when(has_down)
    def _():
        pl.semaphore_signal(barrier, inc=1, device_id={"mesh": me + 1})

    for hop in range(1, n_event):
        pl.semaphore_signal(
            barrier, inc=1, device_id={"event": lax.rem(event + hop, n_event)}
        )

    inputs = (now_ref, before_ref, adj_ref, after_ref)
    for index, ref in enumerate(inputs):
        halo_s[index] = ref[0, :, 0]

    pl.semaphore_wait(
        barrier,
        jnp.where(has_up, 1, 0) + jnp.where(has_down, 1, 0) + (n_event - 1),
    )

    def up_copy(source, target, slot):
        return pltpu.make_async_remote_copy(
            src_ref=source, dst_ref=target, send_sem=s_up.at[slot],
            recv_sem=r_up.at[slot], device_id={"mesh": me - 1},
        )

    def down_copy(source, target, slot):
        return pltpu.make_async_remote_copy(
            src_ref=source, dst_ref=target, send_sem=s_down.at[slot],
            recv_sem=r_down.at[slot], device_id={"mesh": me + 1},
        )

    halo_slot = steps * 2 + 1

    @pl.when(has_up)
    def _():
        up_copy(halo_s, halo_r, halo_slot).start()

    @pl.when(jnp.logical_not(has_down))
    def _():
        halo_r[...] = jnp.zeros_like(halo_r)
        up_r[...] = jnp.zeros_like(up_r)

    @pl.when(jnp.logical_not(has_up))
    def _():
        down_r[...] = jnp.zeros_like(down_r)

    low_half = lane_iota(4) < 64

    def send_faces(top, bottom, slot):
        count = top.shape[0]
        for pair in range(2):
            c = 2 * pair
            up_s[slot, 0:count, pair] = pick(
                low_half, top[:, c : c + 1], roll_lane(top[:, c + 1 : c + 2], 64)
            )[:, 0]
            down_s[slot, 0:count, pair] = pick(
                low_half, roll_lane(bottom[:, c : c + 1], 64), bottom[:, c + 1 : c + 2]
            )[:, 0]

        @pl.when(has_up)
        def _():
            up_copy(up_s.at[slot], up_r.at[slot], slot).start()

        @pl.when(has_down)
        def _():
            down_copy(down_s.at[slot], down_r.at[slot], slot).start()

    def finish_faces(top, bottom, slot):
        count = top.shape[0]

        @pl.when(has_down)
        def _():
            up_copy(up_s.at[slot], up_r.at[slot], slot).wait_recv()

        @pl.when(has_up)
        def _():
            down_copy(down_s.at[slot], down_r.at[slot], slot).wait_recv()

        below = []
        above = []
        for pair in range(2):
            packed = up_r[slot, 0:count, pair : pair + 1]
            below += [roll_lane(packed, 64), packed]
            packed = down_r[slot, 0:count, pair : pair + 1]
            above += [packed, roll_lane(packed, 64)]
        below.append(from_right(below[0]))
        above.append(from_right(above[0]))
        below = jnp.concatenate(below, axis=1)
        above = jnp.concatenate(above, axis=1)
        new_top = top + pick(low_half, above, roll_lane(bottom, 64))
        new_bottom = bottom + pick(low_half, roll_lane(top, 64), below)
        return (new_top, new_bottom)

    materials = jnp.concatenate([lam_ref[...], mu_ref[...], rho_ref[...]], axis=1)
    moved = move_left(rows_ref[...], materials)
    cube = cube_ref[...]
    clam[...] = moved[:, 0:128].reshape(5, 5, 8, LANES) * cube
    cmu[...] = moved[:, 128:256].reshape(5, 5, 8, LANES) * cube
    mass = moved[:, 256:384].reshape(5, 5, 8, LANES) * cube
    mass = [assemble_xy(mass[a : a + 1]) for a in range(5)]
    mass_slot = steps * 2
    send_faces(mass[0], mass[4], mass_slot)

    elem = rec_elem_ref[...] - LANES * me
    lanes = lax.broadcasted_iota(jnp.int32, (32, LANES), 1)
    rec_lane = jnp.where(lanes == elem, 1.0, 0.0)
    off = rec_off_ref[0]
    row = off[:, 0:1] * 40 + off[:, 2:3] * 8 + off[:, 1:2]
    rec_rows = jnp.where(lax.broadcasted_iota(jnp.int32, (32, 200), 1) == row, 1.0, 0.0)
    rec_rows = rec_rows.astype(jnp.bfloat16)
    src_row = src_ref[1] * 40 + src_ref[3] * 8 + src_ref[2]
    src_lane = src_ref[0] - LANES * me

    @pl.when(has_down)
    def _():
        up_copy(halo_s, halo_r, halo_slot).wait_recv()

    for index, ref in enumerate(inputs):
        layer0 = ref[0, :, 0:5]
        layer1 = jnp.concatenate([ref[0, :, 4:8], halo_r[index][:, None]], axis=1)
        parts = []
        for layer in (layer0, layer1):
            for shifted in (layer, roll_sub(layer)):
                parts.append(shifted.reshape(120, LANES))
        moved = move_right(jnp.concatenate(parts, axis=1), spread_ref[...])
        for c in range(4):
            fields[index, :, :, c] = moved[:, c * LANES : (c + 1) * LANES].reshape(
                3, 5, 8, LANES
            )
        fields[index, :, :, 4] = from_right(
            moved[:, 0:LANES].reshape(3, 5, 8, LANES)
        )

    top, bottom = finish_faces(mass[0], mass[4], mass_slot)
    real_row = sub_iota(4) < 5
    for a in range(5):
        plane = top if a == 0 else (bottom if a == 4 else mass[a])
        keep = real_row
        if a == 4:
            keep = keep & ((lane_iota(4) < 64) | has_down)
        keep = jnp.broadcast_to(keep, plane.shape)
        safe = jnp.where(keep, plane, 1.0)
        minv[a] = jnp.where(keep, time_step**2 / safe, 0.0)[0]

    def strain_at(index, a):
        plane = fields[index, :, a]
        gx = []
        for c in range(5):
            total = None
            for k in range(5):
                if DERIV[c, k] == 0.0:
                    continue
                term = float(DERIV[c, k]) * plane[:, k]
                total = term if total is None else total + term
            gx.append(total[:, None])
        gx = jnp.concatenate(gx, axis=1)
        gy = None
        gz = None
        for k in range(5):
            row_k = jnp.broadcast_to(plane[:, :, k : k + 1], plane.shape)
            term = dy_ref[0, k] * row_k
            gy = term if gy is None else gy + term
            term = dz_ref[a * 5 + k] * fields[index, :, k]
            gz = term if gz is None else gz + term
        return (
            gx[0],
            gy[1],
            gz[2],
            gy[0] + gx[1],
            gz[0] + gx[2],
            gz[1] + gy[2],
        )

    def add_kernel(strain, a, moment):
        other = [strains[moment, a, i] for i in range(6)]
        div_a = strain[0] + strain[1] + strain[2]
        div_f = other[0] + other[1] + other[2]
        diag = strain[0] * other[0] + strain[1] * other[1] + strain[2] * other[2]
        shear = strain[3] * other[3] + strain[4] * other[4] + strain[5] * other[5]
        lam_part = div_a * div_f
        mu_part = diag + 0.5 * shear
        if moment == steps - 1:
            ksum[0, a] = lam_part
            ksum[1, a] = mu_part
        else:
            ksum[0, a] = ksum[0, a] + lam_part
            ksum[1, a] = ksum[1, a] + mu_part

    def run_step(index, slot, keep_strain, kernel_moment, load, beside):
        def stress_body(a, carry):
            strain = strain_at(index, a)
            lam_div = clam[a] * (strain[0] + strain[1] + strain[2])
            mu_a = cmu[a]
            mu_two = mu_a + mu_a
            for i in range(3):
                stress[i, a] = lam_div + mu_two * strain[i]
                stress[3 + i, a] = mu_a * strain[3 + i]
            if keep_strain is not None:
                for i in range(6):
                    strains[keep_strain, a, i] = strain[i]
            if kernel_moment is not None:
                add_kernel(strain, a, kernel_moment)
            return carry

        lax.fori_loop(0, 5, stress_body, 0)

        def force_body(a, carry):
            along = ((0, 3, 4), (3, 1, 5), (4, 5, 2))
            for comp in range(3):
                sx = stress[along[comp][0], a]
                sy = stress[along[comp][1], a]
                pieces = []
                for c in range(5):
                    total = None
                    for q in range(5):
                        if DERIV[q, c] == 0.0:
                            continue
                        term = float(DERIV[q, c]) * sx[q]
                        total = term if total is None else total + term
                    pieces.append(total[None])
                total = jnp.concatenate(pieces, axis=0)
                for q in range(5):
                    row_q = jnp.broadcast_to(sy[:, q : q + 1], sy.shape)
                    total = total + dy_ref[1, q] * row_q
                    total = total + dz_ref[25 + a * 5 + q] * stress[along[comp][2], q]
                force[comp, a] = total - load(comp, a)
            force[:, a] = assemble_xy(force[:, a])
            return carry

        lax.fori_loop(0, 5, force_body, 0)
        send_faces(force[:, 0], force[:, 4], slot)
        def inner(a, carry):
            fields[index + 1, :, a] = (
                2.0 * fields[index, :, a] - fields[index + 1, :, a]
            ) - minv[a] * force[:, a]
            return carry

        lax.fori_loop(1, 4, inner, 0)
        if beside is not None:
            beside()
        top, bottom = finish_faces(force[:, 0], force[:, 4], slot)
        for a, plane in ((0, top), (4, bottom)):
            fields[index + 1, :, a] = (
                2.0 * fields[index, :, a] - fields[index + 1, :, a]
            ) - minv[a] * plane

    def swap(index):
        def body(a, carry):
            held = fields[index, :, a]
            fields[index, :, a] = fields[index + 1, :, a]
            fields[index + 1, :, a] = held
            return carry

        lax.fori_loop(0, 5, body, 0)

    def record(moment):
        values = jnp.concatenate(
            [fields[0, comp].reshape(200, LANES) for comp in range(3)], axis=1
        )
        at_rows = move_left(rec_rows, values)
        found = []
        for comp in range(3):
            seen = at_rows[:, comp * LANES : (comp + 1) * LANES] * rec_lane
            found.append(
                jnp.sum(seen, axis=1, keepdims=True)
                - data_ref[0, moment, :, comp : comp + 1]
            )
        return found

    residuals = []

    for moment in range(steps):
        def source_load(comp, a, moment=moment):
            here = (lax.broadcasted_iota(jnp.int32, (5, 8, LANES), 0) * 8
                    + lax.broadcasted_iota(jnp.int32, (5, 8, LANES), 1)
                    + a * 40) == src_row
            there = lax.broadcasted_iota(jnp.int32, (5, 8, LANES), 2) == src_lane
            return jnp.where(here & there, force_ref[moment * 3 + comp], 0.0)

        def beside(moment=moment):
            if moment > 0:
                residuals.append(record(moment - 1))

        run_step(
            0, moment, moment - 1 if moment > 0 else None, None, source_load, beside
        )
        swap(0)
    residuals.append(record(steps - 1))

    def last_strain(a, carry):
        strain = strain_at(0, a)
        for i in range(6):
            strains[steps - 1, a, i] = strain[i]
        return carry

    lax.fori_loop(0, 5, last_strain, 0)

    def put_out(index, ref):
        sides = [fields[index, :, 0:4, c].reshape(96, LANES) for c in range(4)]
        moved = move_right(jnp.concatenate(sides, axis=1), gather_ref[...])
        for ez in range(2):
            first = moved[:, 2 * ez * LANES : (2 * ez + 1) * LANES]
            second = moved[:, (2 * ez + 1) * LANES : (2 * ez + 2) * LANES]
            first = first.reshape(3, 4, 8, LANES)
            second = roll_sub(second.reshape(3, 4, 8, LANES))
            ref[0, :, 4 * ez : 4 * ez + 4] = pick(sub_iota(4) < 4, first, second)

    for moment in reversed(range(steps)):
        scaled = jnp.concatenate(
            [adjoint_gain * residuals[moment][comp] * rec_lane for comp in range(3)],
            axis=1,
        )
        high, middle, low = split3(scaled)
        contract = (((0,), (0,)), ((), ()))
        spreaded = sum(
            lax.dot_general(
                rec_rows, part, contract, preferred_element_type=jnp.float32
            )
            for part in (high, middle, low)
        )
        for comp in range(3):
            clamped = spreaded[:, comp * LANES : (comp + 1) * LANES]
            ev_load = clamped.reshape(5, 5, 8, LANES)
            force[comp] = ev_load

        def beside(moment=moment):
            if moment == steps - 1:
                put_out(0, final_f_ref)

        run_step(
            2,
            2 * steps - 1 - moment,
            None,
            moment,
            lambda comp, a: force[comp, a],
            beside,
        )
        swap(2)

    both = jnp.concatenate(
        [ksum[0].reshape(200, LANES), ksum[1].reshape(200, LANES)], axis=1
    )
    natural = move_left(rows_t_ref[...], both)
    width = LANES // n_event
    k_lam = natural[:, 0:LANES] * (-time_step * lam_ref[...])
    k_mu = natural[:, LANES : 2 * LANES] * (-2.0 * time_step * mu_ref[...])
    lane2 = lax.broadcasted_iota(jnp.int32, (125, LANES), 1)

    def packed_for(target):
        shift = lax.rem(LANES - width * target, LANES)
        return jnp.where(
            lane2 < width,
            pltpu.roll(k_lam, shift, 1),
            pltpu.roll(k_mu, lax.rem(shift + width, LANES), 1),
        )

    def event_copy(hop):
        return pltpu.make_async_remote_copy(
            src_ref=ev_s.at[hop - 1], dst_ref=ev_r.at[hop - 1],
            send_sem=s_ev.at[hop - 1], recv_sem=r_ev.at[hop - 1],
            device_id={"event": lax.rem(event + hop, n_event)},
        )

    for hop in range(1, n_event):
        ev_s[hop - 1] = packed_for(lax.rem(event + hop, n_event))
        event_copy(hop).start()
    put_out(2, final_a_ref)
    total = packed_for(event)
    for hop in range(1, n_event):
        event_copy(hop).wait_recv()
        total = total + ev_r[hop - 1]
    out_ref[0] = total[:, 0:width]
    out_ref[1] = total[:, width : 2 * width]

    @pl.when(has_up)
    def _():
        up_copy(halo_s, halo_r, halo_slot).wait_send()
        for slot in range(2 * steps + 1):
            up_copy(up_s.at[slot], up_r.at[slot], slot).wait_send()

    @pl.when(has_down)
    def _():
        for slot in range(2 * steps + 1):
            down_copy(down_s.at[slot], down_r.at[slot], slot).wait_send()

    for hop in range(1, n_event):
        event_copy(hop).wait_send()


def on_device(
    n_mesh,
    n_event,
    forward_before,
    forward_now,
    adjoint_after,
    adjoint_now,
    mass_density,
    lame_lambda,
    lame_mu,
    source_element,
    source_offset,
    source_force,
    receiver_element,
    receiver_offset,
    receiver_data,
):
    assert forward_now.shape[1:] == (3, 8, 8, 128)
    assert lame_mu.shape == (125, 128)
    steps = source_force.shape[1]
    source = jnp.concatenate([source_element, source_offset[0]])
    field = forward_now.shape
    vmem = pl.BlockSpec(memory_space=pltpu.VMEM)
    smem = pl.BlockSpec(memory_space=pltpu.SMEM)
    f32 = jnp.float32
    elem = (5, 5, 8, LANES)
    slots = 2 * steps + 1
    return pl.pallas_call(
        functools.partial(kernel, n_mesh, n_event, steps),
        out_shape=(
            jax.ShapeDtypeStruct(field, f32),
            jax.ShapeDtypeStruct(field, f32),
            jax.ShapeDtypeStruct((2, 125, LANES // n_event), f32),
        ),
        in_specs=[vmem] * 7 + [smem, smem] + [vmem] * 3 + [vmem] * 6 + [smem],
        out_specs=(vmem, vmem, vmem),
        scratch_shapes=[
            pltpu.VMEM((4, 3) + elem, f32),
            pltpu.VMEM((6,) + elem, f32),
            pltpu.VMEM((3,) + elem, f32),
            pltpu.VMEM((steps, 5, 6, 5, 8, LANES), f32),
            pltpu.VMEM((2,) + elem, f32),
            pltpu.VMEM(elem, f32),
            pltpu.VMEM(elem, f32),
            pltpu.VMEM(elem, f32),
            pltpu.VMEM((4, 3, 8, LANES), f32),
            pltpu.VMEM((4, 3, 8, LANES), f32),
            pltpu.VMEM((slots, 3, 2, 8, LANES), f32),
            pltpu.VMEM((slots, 3, 2, 8, LANES), f32),
            pltpu.VMEM((slots, 3, 2, 8, LANES), f32),
            pltpu.VMEM((slots, 3, 2, 8, LANES), f32),
            pltpu.VMEM((max(1, n_event - 1), 125, LANES), f32),
            pltpu.VMEM((max(1, n_event - 1), 125, LANES), f32),
            pltpu.SemaphoreType.DMA((slots + 1,)),
            pltpu.SemaphoreType.DMA((slots + 1,)),
            pltpu.SemaphoreType.DMA((slots,)),
            pltpu.SemaphoreType.DMA((slots,)),
            pltpu.SemaphoreType.DMA((max(1, n_event - 1),)),
            pltpu.SemaphoreType.DMA((max(1, n_event - 1),)),
        ],
        compiler_params=pltpu.CompilerParams(
            collective_id=0, has_side_effects=True, vmem_limit_bytes=48 * 1024 * 1024
        ),
    )(
        forward_now,
        forward_before,
        adjoint_now,
        adjoint_after,
        mass_density,
        lame_lambda,
        lame_mu,
        source,
        source_force.reshape(-1),
        receiver_element.reshape(-1, 1),
        receiver_offset,
        receiver_data,
        *constants(),
    )


def solution(mesh):
    return jax.shard_map(
        functools.partial(on_device, mesh.shape["mesh"], mesh.shape["event"]),
        mesh=mesh,
        in_specs=(
            P("event", None, "mesh", None, None),
            P("event", None, "mesh", None, None),
            P("event", None, "mesh", None, None),
            P("event", None, "mesh", None, None),
            P(None, "mesh"),
            P(None, "mesh"),
            P(None, "mesh"),
            P("event"),
            P("event", None),
            P("event", None, None),
            P("event", None),
            P("event", None, None),
            P("event", None, None, None),
        ),
        out_specs=(
            P("event", None, "mesh", None, None),
            P("event", None, "mesh", None, None),
            P(None, None, ("mesh", "event")),
        ),
        check_vma=False,
    )
```

```python
import functools
import math

import jax
import jax.numpy as jnp
import numpy as np
from jax import lax
from jax.experimental import pallas as pl
from jax.experimental.pallas import tpu as pltpu
from jax.sharding import PartitionSpec as P

time_step = 0.04
adjoint_gain = 25.0
LANES = 128


def numpy_tables():
    gll_points = np.array([-1.0, -math.sqrt(3.0 / 7.0), 0.0, math.sqrt(3.0 / 7.0), 1.0])
    legendre = (35.0 * gll_points**4 - 30.0 * gll_points**2 + 3.0) / 8.0
    deriv_table = np.zeros((5, 5))
    for row_q in range(5):
        for col_k in range(5):
            if row_q != col_k:
                deriv_table[row_q, col_k] = legendre[row_q] / (
                    legendre[col_k] * (gll_points[row_q] - gll_points[col_k])
                )
    deriv_table[0, 0] = -5.0
    deriv_table[4, 4] = 5.0
    gll_weights = np.array([0.1, 49.0 / 90.0, 32.0 / 45.0, 49.0 / 90.0, 0.1])
    return (deriv_table, gll_weights)


DERIV, WEIGHTS = numpy_tables()


def constants():
    spread = np.zeros((4, LANES, 4, 4, 32), np.float32)
    for j in range(4):
        for ex in range(32):
            for c in range(4):
                spread[j, 4 * ex + c, c, j, ex] = 1.0
    spread = spread.reshape(512, 512)
    rows = np.zeros((5, 5, 8, 125), np.float32)
    cube = np.zeros((5, 5, 8, LANES), np.float32)
    for a in range(5):
        for b in range(5):
            for c in range(5):
                rows[a, c, b, (a * 5 + b) * 5 + c] = 1.0
                cube[a, c, b, :] = WEIGHTS[a] * WEIGHTS[b] * WEIGHTS[c]
    rows = rows.reshape(200, 125)
    dy = np.zeros((2, 5, 8, LANES), np.float32)
    for k in range(5):
        for b in range(5):
            dy[0, k, b, :] = DERIV[b, k]
            dy[1, k, b, :] = DERIV[k, b]
    dz = np.stack([DERIV, DERIV.T]).reshape(-1).astype(np.float32)
    bf = jnp.bfloat16
    return (
        jnp.asarray(spread, bf),
        jnp.asarray(np.ascontiguousarray(spread.T), bf),
        jnp.asarray(rows, bf),
        jnp.asarray(cube),
        jnp.asarray(dy),
        jnp.asarray(dz),
    )


def split3(value):
    high = value.astype(jnp.bfloat16)
    rest = value - high.astype(jnp.float32)
    middle = rest.astype(jnp.bfloat16)
    low = (rest - middle.astype(jnp.float32)).astype(jnp.bfloat16)
    return (high, middle, low)


def dot(left, right):
    return jnp.dot(left, right, preferred_element_type=jnp.float32)


def move_right(values, table):
    parts = split3(values)
    count = values.shape[0]
    stacked = jnp.concatenate(parts, axis=0)
    moved = dot(stacked, table)
    return moved[0:count] + moved[count : 2 * count] + moved[2 * count : 3 * count]


def move_left(table, values):
    high, middle, low = split3(values)
    return dot(table, high) + dot(table, middle) + dot(table, low)


def move_left_t(table, values):
    contract = (((0,), (0,)), ((), ()))
    return sum(
        lax.dot_general(table, part, contract, preferred_element_type=jnp.float32)
        for part in split3(values)
    )


def roll_lane(value, shift):
    return pltpu.roll(value, shift % LANES, value.ndim - 1)


def lane_iota(ndim):
    return lax.broadcasted_iota(jnp.int32, (1,) * (ndim - 1) + (LANES,), ndim - 1)


def sub_iota(ndim):
    return lax.broadcasted_iota(jnp.int32, (1,) * (ndim - 2) + (8, LANES), ndim - 2)


def pick(mask, first, second):
    return jnp.where(jnp.broadcast_to(mask, first.shape), first, second)


def from_left(value):
    at_edge = lane_iota(value.ndim) % 32 == 0
    return pick(at_edge, roll_lane(value, -31), roll_lane(value, 1))


def from_right(value):
    at_edge = lane_iota(value.ndim) % 32 == 31
    return pick(at_edge, roll_lane(value, 31), roll_lane(value, -1))


def roll_sub(value):
    return pltpu.roll(value, 4, value.ndim - 2)


def assemble_xy(value):
    first = value[:, 0:1] + from_left(value[:, 4:5])
    value = jnp.concatenate([first, value[:, 1:4], from_right(first)], axis=1)
    swapped = roll_sub(value)
    other = pick(
        lane_iota(4) % 64 < 32, roll_lane(swapped, -32), roll_lane(swapped, 32)
    )
    return value + pick(sub_iota(4) % 4 == 0, other, jnp.zeros_like(other))


def kernel(
    n_mesh,
    n_event,
    steps,
    now_hbm,
    before_hbm,
    adj_hbm,
    after_hbm,
    rho_hbm,
    lam_hbm,
    mu_hbm,
    rec_elem_hbm,
    rec_off_hbm,
    data_hbm,
    spread_hbm,
    gather_hbm,
    rows_hbm,
    cube_hbm,
    dy_hbm,
    elem_ref,
    off_ref,
    force_ref,
    dz_ref,
    final_f_ref,
    final_a_ref,
    out_ref,
    now_ref,
    before_ref,
    adj_ref,
    after_ref,
    rho_ref,
    lam_ref,
    mu_ref,
    rec_elem_ref,
    rec_off_ref,
    data_ref,
    spread_ref,
    gather_ref,
    rows_ref,
    cube_ref,
    dy_ref,
    s_in,
    fields,
    stress,
    force,
    strains,
    astrain,
    ksum,
    clam,
    cmu,
    minv,
    halo_s,
    halo_r,
    up_s,
    up_r,
    down_s,
    down_r,
    ev_s,
    ev_r,
    s_up,
    r_up,
    s_down,
    r_down,
    s_ev,
    r_ev,
):
    me = lax.axis_index("mesh")
    event = lax.axis_index("event")
    has_up = me > 0
    has_down = me < n_mesh - 1

    loads = []
    pairs = (
        (now_hbm, now_ref),
        (before_hbm, before_ref),
        (adj_hbm, adj_ref),
        (after_hbm, after_ref),
        (rows_hbm, rows_ref),
        (lam_hbm, lam_ref),
        (mu_hbm, mu_ref),
        (rho_hbm, rho_ref),
        (cube_hbm, cube_ref),
        (spread_hbm, spread_ref),
        (dy_hbm, dy_ref),
        (rec_elem_hbm, rec_elem_ref),
        (rec_off_hbm, rec_off_ref),
        (data_hbm, data_ref),
        (gather_hbm, gather_ref),
    )
    for place, (source, target) in enumerate(pairs):
        load_copy = pltpu.make_async_copy(source, target, s_in.at[place])
        load_copy.start()
        loads.append(load_copy)

    barrier = pltpu.get_barrier_semaphore()

    @pl.when(has_up)
    def _():
        pl.semaphore_signal(barrier, inc=1, device_id={"mesh": me - 1})

    @pl.when(has_down)
    def _():
        pl.semaphore_signal(barrier, inc=1, device_id={"mesh": me + 1})

    for hop in range(1, n_event):
        pl.semaphore_signal(
            barrier, inc=1, device_id={"event": lax.rem(event + hop, n_event)}
        )

    inputs = (now_ref, before_ref, adj_ref, after_ref)
    for place in range(4):
        loads[place].wait()
    for index, ref in enumerate(inputs):
        halo_s[index] = ref[0, :, 0]

    pl.semaphore_wait(
        barrier,
        jnp.where(has_up, 1, 0) + jnp.where(has_down, 1, 0) + (n_event - 1),
    )

    def up_copy(source, target, slot):
        return pltpu.make_async_remote_copy(
            src_ref=source, dst_ref=target, send_sem=s_up.at[slot],
            recv_sem=r_up.at[slot], device_id={"mesh": me - 1},
        )

    def down_copy(source, target, slot):
        return pltpu.make_async_remote_copy(
            src_ref=source, dst_ref=target, send_sem=s_down.at[slot],
            recv_sem=r_down.at[slot], device_id={"mesh": me + 1},
        )

    halo_slot = steps * 2 + 1

    @pl.when(has_up)
    def _():
        up_copy(halo_s, halo_r, halo_slot).start()

    @pl.when(jnp.logical_not(has_down))
    def _():
        halo_r[...] = jnp.zeros_like(halo_r)
        up_r[...] = jnp.zeros_like(up_r)

    @pl.when(jnp.logical_not(has_up))
    def _():
        down_r[...] = jnp.zeros_like(down_r)

    low_half = lane_iota(4) < 64

    def send_faces(top, bottom, slot):
        count = top.shape[0]
        for pair in range(2):
            c = 2 * pair
            up_s[slot, 0:count, pair] = pick(
                low_half, top[:, c : c + 1], roll_lane(top[:, c + 1 : c + 2], 64)
            )[:, 0]
            down_s[slot, 0:count, pair] = pick(
                low_half, roll_lane(bottom[:, c : c + 1], 64), bottom[:, c + 1 : c + 2]
            )[:, 0]

        @pl.when(has_up)
        def _():
            up_copy(up_s.at[slot], up_r.at[slot], slot).start()

        @pl.when(has_down)
        def _():
            down_copy(down_s.at[slot], down_r.at[slot], slot).start()

    def finish_faces(top, bottom, slot):
        count = top.shape[0]

        @pl.when(has_down)
        def _():
            up_copy(up_s.at[slot], up_r.at[slot], slot).wait_recv()

        @pl.when(has_up)
        def _():
            down_copy(down_s.at[slot], down_r.at[slot], slot).wait_recv()

        below = []
        above = []
        for pair in range(2):
            packed = up_r[slot, 0:count, pair : pair + 1]
            below += [roll_lane(packed, 64), packed]
            packed = down_r[slot, 0:count, pair : pair + 1]
            above += [packed, roll_lane(packed, 64)]
        below.append(from_right(below[0]))
        above.append(from_right(above[0]))
        below = jnp.concatenate(below, axis=1)
        above = jnp.concatenate(above, axis=1)
        new_top = top + pick(low_half, above, roll_lane(bottom, 64))
        new_bottom = bottom + pick(low_half, roll_lane(top, 64), below)
        return (new_top, new_bottom)

    for place in range(4, 9):
        loads[place].wait()
    materials = jnp.concatenate([lam_ref[...], mu_ref[...], rho_ref[...]], axis=1)
    moved = move_left(rows_ref[...], materials)
    cube = cube_ref[...]
    clam[...] = moved[:, 0:128].reshape(5, 5, 8, LANES) * cube
    cmu[...] = moved[:, 128:256].reshape(5, 5, 8, LANES) * cube
    mass = moved[:, 256:384].reshape(5, 5, 8, LANES) * cube
    mass = [assemble_xy(mass[a : a + 1]) for a in range(5)]
    mass_slot = steps * 2
    send_faces(mass[0], mass[4], mass_slot)

    for place in range(9, 14):
        loads[place].wait()
    nrec = rec_elem_ref.shape[1]
    elem = rec_elem_ref[...] - LANES * me
    lane_t = lax.broadcasted_iota(jnp.int32, (LANES, nrec), 0) == elem
    lane_t = jnp.where(lane_t, 1.0, 0.0).astype(jnp.bfloat16)
    eye = jnp.where(
        lax.broadcasted_iota(jnp.int32, (nrec, nrec), 0)
        == lax.broadcasted_iota(jnp.int32, (nrec, nrec), 1),
        1.0,
        0.0,
    ).astype(jnp.bfloat16)
    turned = (((1,), (1,)), ((), ()))

    def turn(part):
        return lax.dot_general(eye, part, turned, preferred_element_type=jnp.float32)

    rec_lane = turn(lane_t)
    row = rec_off_ref[0] * 40 + rec_off_ref[2] * 8 + rec_off_ref[1]
    rows_lanes = lax.broadcasted_iota(jnp.int32, (200, nrec), 0) == row
    rows_lanes = jnp.where(rows_lanes, 1.0, 0.0).astype(jnp.bfloat16)
    rec_rows = turn(rows_lanes).astype(jnp.bfloat16)
    observed = jnp.concatenate(
        [data_ref[n, comp] for n in range(steps) for comp in range(3)], axis=0
    )
    observed = sum(turn(part) for part in split3(observed))
    src_row = off_ref[0, 0] * 40 + off_ref[0, 2] * 8 + off_ref[0, 1]
    src_lane = elem_ref[0] - LANES * me

    @pl.when(has_down)
    def _():
        up_copy(halo_s, halo_r, halo_slot).wait_recv()

    def bring_in(index):
        ref = inputs[index]
        layer0 = ref[0, :, 0:5]
        layer1 = jnp.concatenate([ref[0, :, 4:8], halo_r[index][:, None]], axis=1)
        parts = []
        for layer in (layer0, layer1):
            for shifted in (layer, roll_sub(layer)):
                parts.append(shifted.reshape(120, LANES))
        moved = move_right(jnp.concatenate(parts, axis=1), spread_ref[...])
        for c in range(4):
            fields[index, :, :, c] = moved[:, c * LANES : (c + 1) * LANES].reshape(
                3, 5, 8, LANES
            )
        fields[index, :, :, 4] = from_right(
            moved[:, 0:LANES].reshape(3, 5, 8, LANES)
        )

    def finish_mass():
        top, bottom = finish_faces(mass[0], mass[4], mass_slot)
        real_row = sub_iota(4) < 5
        for a in range(5):
            plane = top if a == 0 else (bottom if a == 4 else mass[a])
            keep = real_row
            if a == 4:
                keep = keep & ((lane_iota(4) < 64) | has_down)
            keep = jnp.broadcast_to(keep, plane.shape)
            safe = jnp.where(keep, plane, 1.0)
            minv[a] = jnp.where(keep, time_step**2 / safe, 0.0)[0]

    bring_in(0)

    def strain_at(index, a):
        plane = fields[index, :, a]
        gx = []
        for c in range(5):
            total = None
            for k in range(5):
                if DERIV[c, k] == 0.0:
                    continue
                term = float(DERIV[c, k]) * plane[:, k]
                total = term if total is None else total + term
            gx.append(total[:, None])
        gx = jnp.concatenate(gx, axis=1)
        gy = None
        gz = None
        for k in range(5):
            row_k = jnp.broadcast_to(plane[:, :, k : k + 1], plane.shape)
            term = dy_ref[0, k] * row_k
            gy = term if gy is None else gy + term
            term = dz_ref[a * 5 + k] * fields[index, :, k]
            gz = term if gz is None else gz + term
        return (
            gx[0],
            gy[1],
            gz[2],
            gy[0] + gx[1],
            gz[0] + gx[2],
            gz[1] + gy[2],
        )

    def add_kernels(moment, last_index):
        def body(a, carry):
            strain = [astrain[a, i] for i in range(6)]
            if last_index is None:
                other = [strains[moment, a, i] for i in range(6)]
            else:
                other = strain_at(last_index, a)
            div_a = strain[0] + strain[1] + strain[2]
            div_f = other[0] + other[1] + other[2]
            diag = strain[0] * other[0] + strain[1] * other[1] + strain[2] * other[2]
            shear = strain[3] * other[3] + strain[4] * other[4] + strain[5] * other[5]
            lam_part = div_a * div_f
            mu_part = diag + 0.5 * shear
            if last_index is not None:
                ksum[0, a] = lam_part
                ksum[1, a] = mu_part
            else:
                ksum[0, a] = ksum[0, a] + lam_part
                ksum[1, a] = ksum[1, a] + mu_part
            return carry

        lax.fori_loop(0, 5, body, 0)

    def run_step(index, older, slot, keep_strain, load, beside):
        def stress_body(a, carry):
            strain = strain_at(index, a)
            lam_div = clam[a] * (strain[0] + strain[1] + strain[2])
            mu_a = cmu[a]
            mu_two = mu_a + mu_a
            for i in range(3):
                stress[i, a] = lam_div + mu_two * strain[i]
                stress[3 + i, a] = mu_a * strain[3 + i]
            if keep_strain is not None:
                for i in range(6):
                    keep_strain[a, i] = strain[i]
            return carry

        lax.fori_loop(0, 5, stress_body, 0)

        def force_body(a, carry):
            along = ((0, 3, 4), (3, 1, 5), (4, 5, 2))
            for comp in range(3):
                sx = stress[along[comp][0], a]
                sy = stress[along[comp][1], a]
                pieces = []
                for c in range(5):
                    total = None
                    for q in range(5):
                        if DERIV[q, c] == 0.0:
                            continue
                        term = float(DERIV[q, c]) * sx[q]
                        total = term if total is None else total + term
                    pieces.append(total[None])
                total = jnp.concatenate(pieces, axis=0)
                for q in range(5):
                    row_q = jnp.broadcast_to(sy[:, q : q + 1], sy.shape)
                    total = total + dy_ref[1, q] * row_q
                    total = total + dz_ref[25 + a * 5 + q] * stress[along[comp][2], q]
                force[comp, a] = total - load(comp, a)
            force[:, a] = assemble_xy(force[:, a])
            return carry

        lax.fori_loop(0, 5, force_body, 0)
        send_faces(force[:, 0], force[:, 4], slot)
        beside()

        def inner(a, carry):
            fields[older, :, a] = (
                2.0 * fields[index, :, a] - fields[older, :, a]
            ) - minv[a] * force[:, a]
            return carry

        lax.fori_loop(1, 4, inner, 0)
        top, bottom = finish_faces(force[:, 0], force[:, 4], slot)
        for a, plane in ((0, top), (4, bottom)):
            fields[older, :, a] = (
                2.0 * fields[index, :, a] - fields[older, :, a]
            ) - minv[a] * plane

    def record(index, moment):
        values = jnp.concatenate(
            [fields[index, comp].reshape(200, LANES) for comp in range(3)], axis=1
        )
        at_rows = move_left(rec_rows, values)
        found = []
        for comp in range(3):
            seen = at_rows[:, comp * LANES : (comp + 1) * LANES] * rec_lane
            found.append(
                jnp.sum(seen, axis=1, keepdims=True)
                - observed[:, 3 * moment + comp : 3 * moment + comp + 1]
            )
        return found

    residuals = []

    index, older = 0, 1
    for moment in range(steps):
        def source_load(comp, a, moment=moment):
            here = (lax.broadcasted_iota(jnp.int32, (5, 8, LANES), 0) * 8
                    + lax.broadcasted_iota(jnp.int32, (5, 8, LANES), 1)
                    + a * 40) == src_row
            there = lax.broadcasted_iota(jnp.int32, (5, 8, LANES), 2) == src_lane
            return jnp.where(here & there, force_ref[moment, 0, comp], 0.0)

        def beside(moment=moment, index=index):
            if moment == 0:
                bring_in(1)
                finish_mass()
            else:
                residuals.append(record(index, moment - 1))
            if moment == min(1, steps - 1):
                bring_in(2)
            if moment == steps - 1:
                bring_in(3)

        run_step(
            index,
            older,
            moment,
            strains.at[moment - 1] if moment > 0 else None,
            source_load,
            beside,
        )
        index, older = older, index
    residuals.append(record(index, steps - 1))
    last_forward = index
    loads[14].wait()

    def put_out(index, ref):
        sides = [fields[index, :, 0:4, c].reshape(96, LANES) for c in range(4)]
        moved = move_right(jnp.concatenate(sides, axis=1), gather_ref[...])
        for ez in range(2):
            first = moved[:, 2 * ez * LANES : (2 * ez + 1) * LANES]
            second = moved[:, (2 * ez + 1) * LANES : (2 * ez + 2) * LANES]
            first = first.reshape(3, 4, 8, LANES)
            second = roll_sub(second.reshape(3, 4, 8, LANES))
            ref[0, :, 4 * ez : 4 * ez + 4] = pick(sub_iota(4) < 4, first, second)

    width = LANES // n_event

    def event_copy(hop):
        target = lax.rem(event + hop, n_event)
        return pltpu.make_async_remote_copy(
            src_ref=ev_s.at[:, pl.ds(pl.multiple_of(width * target, width), width)],
            dst_ref=ev_r.at[hop - 1],
            send_sem=s_ev.at[hop - 1],
            recv_sem=r_ev.at[hop - 1],
            device_id={"event": target},
        )

    def send_kernels():
        scales = (-time_step, -2.0 * time_step)
        for which, modulus in enumerate((lam_ref, mu_ref)):
            natural = move_left_t(rows_ref[...], ksum[which].reshape(200, LANES))
            ev_s[which] = jnp.transpose(natural * (scales[which] * modulus[...]))
        for hop in range(1, n_event):
            event_copy(hop).start()

    index, older = 2, 3
    for moment in reversed(range(steps)):
        scaled = jnp.concatenate(
            [adjoint_gain * residuals[moment][comp] * rec_lane for comp in range(3)],
            axis=1,
        )
        injected = sum(dot(rows_lanes, part) for part in split3(scaled))
        for comp in range(3):
            force[comp] = injected[:, comp * LANES : (comp + 1) * LANES].reshape(
                5, 5, 8, LANES
            )

        def beside(moment=moment):
            add_kernels(moment, last_forward if moment == steps - 1 else None)
            if moment == steps - 1:
                put_out(last_forward, final_f_ref)
            if moment == 0:
                send_kernels()

        run_step(
            index,
            older,
            2 * steps - 1 - moment,
            astrain,
            lambda comp, a: force[comp, a],
            beside,
        )
        index, older = older, index

    put_out(index, final_a_ref)
    mine = pl.ds(pl.multiple_of(width * event, width), width)
    total = ev_s[:, mine]
    for hop in range(1, n_event):
        event_copy(hop).wait_recv()
        total = total + ev_r[hop - 1]
    out_ref[...] = total

    @pl.when(has_up)
    def _():
        up_copy(halo_s, halo_r, halo_slot).wait_send()
        for slot in range(2 * steps + 1):
            up_copy(up_s.at[slot], up_r.at[slot], slot).wait_send()

    @pl.when(has_down)
    def _():
        for slot in range(2 * steps + 1):
            down_copy(down_s.at[slot], down_r.at[slot], slot).wait_send()

    for hop in range(1, n_event):
        event_copy(hop).wait_send()


def on_device(
    n_mesh,
    n_event,
    forward_before,
    forward_now,
    adjoint_after,
    adjoint_now,
    mass_density,
    lame_lambda,
    lame_mu,
    source_element,
    source_offset,
    source_force,
    receiver_element,
    receiver_offset,
    receiver_data,
):
    assert forward_now.shape[1:] == (3, 8, 8, 128)
    assert lame_mu.shape == (125, 128)
    steps = source_force.shape[1]
    field = forward_now.shape
    vmem = pl.BlockSpec(memory_space=pltpu.VMEM)
    hbm = pl.BlockSpec(memory_space=pltpu.HBM)
    smem = pl.BlockSpec(memory_space=pltpu.SMEM)
    f32 = jnp.float32
    elem = (5, 5, 8, LANES)
    slots = 2 * steps + 1
    copied = (
        forward_now,
        forward_before,
        adjoint_now,
        adjoint_after,
        mass_density,
        lame_lambda,
        lame_mu,
        receiver_element,
        receiver_offset.transpose(2, 0, 1),
        receiver_data.transpose(1, 3, 0, 2),
    ) + constants()[:-1]
    final_f, final_a, kernels = pl.pallas_call(
        functools.partial(kernel, n_mesh, n_event, steps),
        out_shape=(
            jax.ShapeDtypeStruct(field, f32),
            jax.ShapeDtypeStruct(field, f32),
            jax.ShapeDtypeStruct((2, LANES // n_event, 125), f32),
        ),
        in_specs=[hbm] * 15 + [smem] * 4,
        out_specs=(vmem, vmem, vmem),
        scratch_shapes=[pltpu.VMEM(value.shape, value.dtype) for value in copied]
        + [
            pltpu.SemaphoreType.DMA((len(copied),)),
            pltpu.VMEM((4, 3) + elem, f32),
            pltpu.VMEM((6,) + elem, f32),
            pltpu.VMEM((3,) + elem, f32),
            pltpu.VMEM((steps, 5, 6, 5, 8, LANES), f32),
            pltpu.VMEM((5, 6, 5, 8, LANES), f32),
            pltpu.VMEM((2,) + elem, f32),
            pltpu.VMEM(elem, f32),
            pltpu.VMEM(elem, f32),
            pltpu.VMEM(elem, f32),
            pltpu.VMEM((4, 3, 8, LANES), f32),
            pltpu.VMEM((4, 3, 8, LANES), f32),
            pltpu.VMEM((slots, 3, 2, 8, LANES), f32),
            pltpu.VMEM((slots, 3, 2, 8, LANES), f32),
            pltpu.VMEM((slots, 3, 2, 8, LANES), f32),
            pltpu.VMEM((slots, 3, 2, 8, LANES), f32),
            pltpu.VMEM((2, LANES, 125), f32),
            pltpu.VMEM((max(1, n_event - 1), 2, LANES // n_event, 125), f32),
            pltpu.SemaphoreType.DMA((slots + 1,)),
            pltpu.SemaphoreType.DMA((slots + 1,)),
            pltpu.SemaphoreType.DMA((slots,)),
            pltpu.SemaphoreType.DMA((slots,)),
            pltpu.SemaphoreType.DMA((max(1, n_event - 1),)),
            pltpu.SemaphoreType.DMA((max(1, n_event - 1),)),
        ],
        compiler_params=pltpu.CompilerParams(
            collective_id=0, has_side_effects=True, vmem_limit_bytes=60 * 1024 * 1024
        ),
    )(
        *copied,
        source_element,
        source_offset,
        source_force.transpose(1, 0, 2),
        constants()[-1],
    )
    return (final_f, final_a, kernels.transpose(0, 2, 1))


def solution(mesh):
    return jax.shard_map(
        functools.partial(on_device, mesh.shape["mesh"], mesh.shape["event"]),
        mesh=mesh,
        in_specs=(
            P("event", None, "mesh", None, None),
            P("event", None, "mesh", None, None),
            P("event", None, "mesh", None, None),
            P("event", None, "mesh", None, None),
            P(None, "mesh"),
            P(None, "mesh"),
            P(None, "mesh"),
            P("event"),
            P("event", None),
            P("event", None, None),
            P("event", None),
            P("event", None, None),
            P("event", None, None, None),
        ),
        out_specs=(
            P("event", None, "mesh", None, None),
            P("event", None, "mesh", None, None),
            P(None, None, ("mesh", "event")),
        ),
        check_vma=False,
    )
```

```python
import functools
import math

import jax
import jax.numpy as jnp
import numpy as np
from jax import lax
from jax.experimental import pallas as pl
from jax.experimental.pallas import tpu as pltpu
from jax.sharding import PartitionSpec as P

time_step = 0.04
adjoint_gain = 25.0
LANES = 128


def numpy_tables():
    gll_points = np.array([-1.0, -math.sqrt(3.0 / 7.0), 0.0, math.sqrt(3.0 / 7.0), 1.0])
    legendre = (35.0 * gll_points**4 - 30.0 * gll_points**2 + 3.0) / 8.0
    deriv_table = np.zeros((5, 5))
    for row_q in range(5):
        for col_k in range(5):
            if row_q != col_k:
                deriv_table[row_q, col_k] = legendre[row_q] / (
                    legendre[col_k] * (gll_points[row_q] - gll_points[col_k])
                )
    deriv_table[0, 0] = -5.0
    deriv_table[4, 4] = 5.0
    gll_weights = np.array([0.1, 49.0 / 90.0, 32.0 / 45.0, 49.0 / 90.0, 0.1])
    return (deriv_table, gll_weights)


DERIV, WEIGHTS = numpy_tables()


def constants():
    spread = np.zeros((4, LANES, 4, 4, 32), np.float32)
    for j in range(4):
        for ex in range(32):
            for c in range(4):
                spread[j, 4 * ex + c, c, j, ex] = 1.0
    spread = spread.reshape(512, 512)
    rows = np.zeros((5, 5, 8, 125), np.float32)
    cube = np.zeros((5, 5, 8, LANES), np.float32)
    for a in range(5):
        for b in range(5):
            for c in range(5):
                rows[a, c, b, (a * 5 + b) * 5 + c] = 1.0
                cube[a, c, b, :] = WEIGHTS[a] * WEIGHTS[b] * WEIGHTS[c]
    rows = rows.reshape(200, 125)
    dy = np.zeros((2, 5, 8, LANES), np.float32)
    for k in range(5):
        for b in range(5):
            dy[0, k, b, :] = DERIV[b, k]
            dy[1, k, b, :] = DERIV[k, b]
    bf = jnp.bfloat16
    return (
        jnp.asarray(spread, bf),
        jnp.asarray(np.ascontiguousarray(spread.T), bf),
        jnp.asarray(rows, bf),
        jnp.asarray(cube),
        jnp.asarray(dy),
    )


def split3(value):
    high = value.astype(jnp.bfloat16)
    rest = value - high.astype(jnp.float32)
    middle = rest.astype(jnp.bfloat16)
    low = (rest - middle.astype(jnp.float32)).astype(jnp.bfloat16)
    return (high, middle, low)


def dot(left, right):
    return jnp.dot(left, right, preferred_element_type=jnp.float32)


def move_right(values, table):
    parts = split3(values)
    count = values.shape[0]
    stacked = jnp.concatenate(parts, axis=0)
    moved = dot(stacked, table)
    return moved[0:count] + moved[count : 2 * count] + moved[2 * count : 3 * count]


def move_left(table, values):
    high, middle, low = split3(values)
    return dot(table, high) + dot(table, middle) + dot(table, low)


def move_left_t(table, values):
    contract = (((0,), (0,)), ((), ()))
    return sum(
        lax.dot_general(table, part, contract, preferred_element_type=jnp.float32)
        for part in split3(values)
    )


def roll_lane(value, shift):
    return pltpu.roll(value, shift % LANES, value.ndim - 1)


def lane_iota(ndim):
    return lax.broadcasted_iota(jnp.int32, (1,) * (ndim - 1) + (LANES,), ndim - 1)


def sub_iota(ndim):
    return lax.broadcasted_iota(jnp.int32, (1,) * (ndim - 2) + (8, LANES), ndim - 2)


def pick(mask, first, second):
    return jnp.where(jnp.broadcast_to(mask, first.shape), first, second)


def from_left(value):
    at_edge = lane_iota(value.ndim) % 32 == 0
    return pick(at_edge, roll_lane(value, -31), roll_lane(value, 1))


def from_right(value):
    at_edge = lane_iota(value.ndim) % 32 == 31
    return pick(at_edge, roll_lane(value, 31), roll_lane(value, -1))


def roll_sub(value):
    return pltpu.roll(value, 4, value.ndim - 2)


def assemble_xy(value):
    first = value[:, 0:1] + from_left(value[:, 4:5])
    value = jnp.concatenate([first, value[:, 1:4], from_right(first)], axis=1)
    swapped = roll_sub(value)
    other = pick(
        lane_iota(4) % 64 < 32, roll_lane(swapped, -32), roll_lane(swapped, 32)
    )
    return value + pick(sub_iota(4) % 4 == 0, other, jnp.zeros_like(other))


def each(first, last, body):
    for a in range(first, last):
        body(a, 0)


def kernel(
    n_mesh,
    n_event,
    steps,
    now_hbm,
    before_hbm,
    adj_hbm,
    after_hbm,
    rho_hbm,
    lam_hbm,
    mu_hbm,
    rec_elem_hbm,
    rec_off_hbm,
    data_hbm,
    spread_hbm,
    gather_hbm,
    rows_hbm,
    cube_hbm,
    dy_hbm,
    elem_ref,
    off_ref,
    force_ref,
    final_f_ref,
    final_a_ref,
    out_ref,
    now_ref,
    before_ref,
    adj_ref,
    after_ref,
    rho_ref,
    lam_ref,
    mu_ref,
    rec_elem_ref,
    rec_off_ref,
    data_ref,
    spread_ref,
    gather_ref,
    rows_ref,
    cube_ref,
    dy_ref,
    s_in,
    fields,
    stress,
    force,
    strains,
    astrain,
    ksum,
    clam,
    cmu,
    minv,
    halo_s,
    halo_r,
    up_s,
    up_r,
    down_s,
    down_r,
    ev_s,
    ev_r,
    s_up,
    r_up,
    s_down,
    r_down,
    s_ev,
    r_ev,
):
    me = lax.axis_index("mesh")
    event = lax.axis_index("event")
    has_up = me > 0
    has_down = me < n_mesh - 1

    loads = []
    pairs = (
        (now_hbm, now_ref),
        (before_hbm, before_ref),
        (adj_hbm, adj_ref),
        (after_hbm, after_ref),
        (rows_hbm, rows_ref),
        (lam_hbm, lam_ref),
        (mu_hbm, mu_ref),
        (rho_hbm, rho_ref),
        (cube_hbm, cube_ref),
        (spread_hbm, spread_ref),
        (dy_hbm, dy_ref),
        (rec_elem_hbm, rec_elem_ref),
        (rec_off_hbm, rec_off_ref),
        (data_hbm, data_ref),
        (gather_hbm, gather_ref),
    )
    for place, (source, target) in enumerate(pairs):
        load_copy = pltpu.make_async_copy(source, target, s_in.at[place])
        load_copy.start()
        loads.append(load_copy)

    barrier = pltpu.get_barrier_semaphore()

    @pl.when(has_up)
    def _():
        pl.semaphore_signal(barrier, inc=1, device_id={"mesh": me - 1})

    @pl.when(has_down)
    def _():
        pl.semaphore_signal(barrier, inc=1, device_id={"mesh": me + 1})

    for hop in range(1, n_event):
        pl.semaphore_signal(
            barrier, inc=1, device_id={"event": lax.rem(event + hop, n_event)}
        )

    inputs = (now_ref, before_ref, adj_ref, after_ref)
    for place in range(4):
        loads[place].wait()
    for index, ref in enumerate(inputs):
        halo_s[index] = ref[0, :, 0]

    pl.semaphore_wait(
        barrier,
        jnp.where(has_up, 1, 0) + jnp.where(has_down, 1, 0) + (n_event - 1),
    )

    def up_copy(source, target, slot):
        return pltpu.make_async_remote_copy(
            src_ref=source, dst_ref=target, send_sem=s_up.at[slot],
            recv_sem=r_up.at[slot], device_id={"mesh": me - 1},
        )

    def down_copy(source, target, slot):
        return pltpu.make_async_remote_copy(
            src_ref=source, dst_ref=target, send_sem=s_down.at[slot],
            recv_sem=r_down.at[slot], device_id={"mesh": me + 1},
        )

    halo_slot = steps * 2 + 1

    @pl.when(has_up)
    def _():
        up_copy(halo_s, halo_r, halo_slot).start()

    @pl.when(jnp.logical_not(has_down))
    def _():
        halo_r[...] = jnp.zeros_like(halo_r)
        up_r[...] = jnp.zeros_like(up_r)

    @pl.when(jnp.logical_not(has_up))
    def _():
        down_r[...] = jnp.zeros_like(down_r)

    low_half = lane_iota(4) < 64

    def send_faces(top, bottom, slot):
        count = top.shape[0]
        for pair in range(2):
            c = 2 * pair
            up_s[slot, 0:count, pair] = pick(
                low_half, top[:, c : c + 1], roll_lane(top[:, c + 1 : c + 2], 64)
            )[:, 0]
            down_s[slot, 0:count, pair] = pick(
                low_half, roll_lane(bottom[:, c : c + 1], 64), bottom[:, c + 1 : c + 2]
            )[:, 0]

        @pl.when(has_up)
        def _():
            up_copy(up_s.at[slot], up_r.at[slot], slot).start()

        @pl.when(has_down)
        def _():
            down_copy(down_s.at[slot], down_r.at[slot], slot).start()

    def finish_faces(top, bottom, slot):
        count = top.shape[0]

        @pl.when(has_down)
        def _():
            up_copy(up_s.at[slot], up_r.at[slot], slot).wait_recv()

        @pl.when(has_up)
        def _():
            down_copy(down_s.at[slot], down_r.at[slot], slot).wait_recv()

        below = []
        above = []
        for pair in range(2):
            packed = up_r[slot, 0:count, pair : pair + 1]
            below += [roll_lane(packed, 64), packed]
            packed = down_r[slot, 0:count, pair : pair + 1]
            above += [packed, roll_lane(packed, 64)]
        below.append(from_right(below[0]))
        above.append(from_right(above[0]))
        below = jnp.concatenate(below, axis=1)
        above = jnp.concatenate(above, axis=1)
        new_top = top + pick(low_half, above, roll_lane(bottom, 64))
        new_bottom = bottom + pick(low_half, roll_lane(top, 64), below)
        return (new_top, new_bottom)

    for place in range(4, 9):
        loads[place].wait()
    materials = jnp.concatenate([lam_ref[...], mu_ref[...], rho_ref[...]], axis=1)
    moved = move_left(rows_ref[...], materials)
    cube = cube_ref[...]
    clam[...] = moved[:, 0:128].reshape(5, 5, 8, LANES) * cube
    cmu[...] = moved[:, 128:256].reshape(5, 5, 8, LANES) * cube
    mass = moved[:, 256:384].reshape(5, 5, 8, LANES) * cube
    mass = [assemble_xy(mass[a : a + 1]) for a in range(5)]
    mass_slot = steps * 2
    send_faces(mass[0], mass[4], mass_slot)

    for place in range(9, 14):
        loads[place].wait()
    nrec = rec_elem_ref.shape[1]
    elem = rec_elem_ref[...] - LANES * me
    lane_t = lax.broadcasted_iota(jnp.int32, (LANES, nrec), 0) == elem
    lane_t = jnp.where(lane_t, 1.0, 0.0).astype(jnp.bfloat16)
    eye = jnp.where(
        lax.broadcasted_iota(jnp.int32, (nrec, nrec), 0)
        == lax.broadcasted_iota(jnp.int32, (nrec, nrec), 1),
        1.0,
        0.0,
    ).astype(jnp.bfloat16)
    turned = (((1,), (1,)), ((), ()))

    def turn(part):
        return lax.dot_general(eye, part, turned, preferred_element_type=jnp.float32)

    rec_lane = turn(lane_t)
    row = rec_off_ref[0] * 40 + rec_off_ref[2] * 8 + rec_off_ref[1]
    rows_lanes = lax.broadcasted_iota(jnp.int32, (200, nrec), 0) == row
    rows_lanes = jnp.where(rows_lanes, 1.0, 0.0).astype(jnp.bfloat16)
    rec_rows = turn(rows_lanes).astype(jnp.bfloat16)
    observed = jnp.concatenate(
        [data_ref[n, comp] for n in range(steps) for comp in range(3)], axis=0
    )
    observed = sum(turn(part) for part in split3(observed))
    src_row = off_ref[0, 0] * 40 + off_ref[0, 2] * 8 + off_ref[0, 1]
    src_lane = elem_ref[0] - LANES * me

    @pl.when(has_down)
    def _():
        up_copy(halo_s, halo_r, halo_slot).wait_recv()

    def bring_in(index):
        ref = inputs[index]
        layer0 = ref[0, :, 0:5]
        layer1 = jnp.concatenate([ref[0, :, 4:8], halo_r[index][:, None]], axis=1)
        parts = []
        for layer in (layer0, layer1):
            for shifted in (layer, roll_sub(layer)):
                parts.append(shifted.reshape(120, LANES))
        moved = move_right(jnp.concatenate(parts, axis=1), spread_ref[...])
        for c in range(4):
            fields[index, :, :, c] = moved[:, c * LANES : (c + 1) * LANES].reshape(
                3, 5, 8, LANES
            )
        fields[index, :, :, 4] = from_right(
            moved[:, 0:LANES].reshape(3, 5, 8, LANES)
        )

    def finish_mass():
        top, bottom = finish_faces(mass[0], mass[4], mass_slot)
        real_row = sub_iota(4) < 5
        for a in range(5):
            plane = top if a == 0 else (bottom if a == 4 else mass[a])
            keep = real_row
            if a == 4:
                keep = keep & ((lane_iota(4) < 64) | has_down)
            keep = jnp.broadcast_to(keep, plane.shape)
            safe = jnp.where(keep, plane, 1.0)
            minv[a] = jnp.where(keep, time_step**2 / safe, 0.0)[0]

    bring_in(0)

    def strain_at(index, a):
        plane = fields[index, :, a]
        gx = []
        for c in range(5):
            total = None
            for k in range(5):
                if DERIV[c, k] == 0.0:
                    continue
                term = float(DERIV[c, k]) * plane[:, k]
                total = term if total is None else total + term
            gx.append(total[:, None])
        gx = jnp.concatenate(gx, axis=1)
        gy = None
        gz = None
        for k in range(5):
            row_k = jnp.broadcast_to(plane[:, :, k : k + 1], plane.shape)
            term = dy_ref[0, k] * row_k
            gy = term if gy is None else gy + term
            if DERIV[a, k] != 0.0:
                term = float(DERIV[a, k]) * fields[index, :, k]
                gz = term if gz is None else gz + term
        return (
            gx[0],
            gy[1],
            gz[2],
            gy[0] + gx[1],
            gz[0] + gx[2],
            gz[1] + gy[2],
        )

    def add_kernels(moment, last_index):
        def body(a, carry):
            strain = [astrain[a, i] for i in range(6)]
            if last_index is None:
                other = [strains[moment, a, i] for i in range(6)]
            else:
                other = strain_at(last_index, a)
            div_a = strain[0] + strain[1] + strain[2]
            div_f = other[0] + other[1] + other[2]
            diag = strain[0] * other[0] + strain[1] * other[1] + strain[2] * other[2]
            shear = strain[3] * other[3] + strain[4] * other[4] + strain[5] * other[5]
            lam_part = div_a * div_f
            mu_part = diag + 0.5 * shear
            if last_index is not None:
                ksum[0, a] = lam_part
                ksum[1, a] = mu_part
            else:
                ksum[0, a] = ksum[0, a] + lam_part
                ksum[1, a] = ksum[1, a] + mu_part
            return carry

        each(0, 5, body)

    def run_step(index, older, slot, keep_strain, load, beside):
        def stress_body(a, carry):
            strain = strain_at(index, a)
            lam_div = clam[a] * (strain[0] + strain[1] + strain[2])
            mu_a = cmu[a]
            mu_two = mu_a + mu_a
            for i in range(3):
                stress[i, a] = lam_div + mu_two * strain[i]
                stress[3 + i, a] = mu_a * strain[3 + i]
            if keep_strain is not None:
                for i in range(6):
                    keep_strain[a, i] = strain[i]
            return carry

        each(0, 5, stress_body)

        def force_body(a, carry):
            along = ((0, 3, 4), (3, 1, 5), (4, 5, 2))
            for comp in range(3):
                sx = stress[along[comp][0], a]
                sy = stress[along[comp][1], a]
                pieces = []
                for c in range(5):
                    total = None
                    for q in range(5):
                        if DERIV[q, c] == 0.0:
                            continue
                        term = float(DERIV[q, c]) * sx[q]
                        total = term if total is None else total + term
                    pieces.append(total[None])
                total = jnp.concatenate(pieces, axis=0)
                for q in range(5):
                    row_q = jnp.broadcast_to(sy[:, q : q + 1], sy.shape)
                    total = total + dy_ref[1, q] * row_q
                    if DERIV[q, a] != 0.0:
                        total = total + float(DERIV[q, a]) * stress[along[comp][2], q]
                force[comp, a] = total - load(comp, a)
            force[:, a] = assemble_xy(force[:, a])
            return carry

        each(0, 5, force_body)
        send_faces(force[:, 0], force[:, 4], slot)
        beside()

        def inner(a, carry):
            fields[older, :, a] = (
                2.0 * fields[index, :, a] - fields[older, :, a]
            ) - minv[a] * force[:, a]
            return carry

        each(1, 4, inner)
        top, bottom = finish_faces(force[:, 0], force[:, 4], slot)
        for a, plane in ((0, top), (4, bottom)):
            fields[older, :, a] = (
                2.0 * fields[index, :, a] - fields[older, :, a]
            ) - minv[a] * plane

    def record(index, moment):
        values = jnp.concatenate(
            [fields[index, comp].reshape(200, LANES) for comp in range(3)], axis=1
        )
        at_rows = move_left(rec_rows, values)
        found = []
        for comp in range(3):
            seen = at_rows[:, comp * LANES : (comp + 1) * LANES] * rec_lane
            found.append(
                jnp.sum(seen, axis=1, keepdims=True)
                - observed[:, 3 * moment + comp : 3 * moment + comp + 1]
            )
        return found

    residuals = []

    index, older = 0, 1
    for moment in range(steps):
        def source_load(comp, a, moment=moment):
            here = (lax.broadcasted_iota(jnp.int32, (5, 8, LANES), 0) * 8
                    + lax.broadcasted_iota(jnp.int32, (5, 8, LANES), 1)
                    + a * 40) == src_row
            there = lax.broadcasted_iota(jnp.int32, (5, 8, LANES), 2) == src_lane
            return jnp.where(here & there, force_ref[moment, 0, comp], 0.0)

        def beside(moment=moment, index=index):
            if moment == 0:
                bring_in(1)
                finish_mass()
            else:
                residuals.append(record(index, moment - 1))
            if moment == min(1, steps - 1):
                bring_in(2)
            if moment == steps - 1:
                bring_in(3)

        run_step(
            index,
            older,
            moment,
            strains.at[moment - 1] if moment > 0 else None,
            source_load,
            beside,
        )
        index, older = older, index
    residuals.append(record(index, steps - 1))
    last_forward = index
    loads[14].wait()

    def put_out(index, ref):
        sides = [fields[index, :, 0:4, c].reshape(96, LANES) for c in range(4)]
        moved = move_right(jnp.concatenate(sides, axis=1), gather_ref[...])
        for ez in range(2):
            first = moved[:, 2 * ez * LANES : (2 * ez + 1) * LANES]
            second = moved[:, (2 * ez + 1) * LANES : (2 * ez + 2) * LANES]
            first = first.reshape(3, 4, 8, LANES)
            second = roll_sub(second.reshape(3, 4, 8, LANES))
            ref[0, :, 4 * ez : 4 * ez + 4] = pick(sub_iota(4) < 4, first, second)

    width = LANES // n_event

    def event_copy(hop):
        target = lax.rem(event + hop, n_event)
        return pltpu.make_async_remote_copy(
            src_ref=ev_s.at[:, pl.ds(pl.multiple_of(width * target, width), width)],
            dst_ref=ev_r.at[hop - 1],
            send_sem=s_ev.at[hop - 1],
            recv_sem=r_ev.at[hop - 1],
            device_id={"event": target},
        )

    def send_kernels():
        scales = (-time_step, -2.0 * time_step)
        for which, modulus in enumerate((lam_ref, mu_ref)):
            natural = move_left_t(rows_ref[...], ksum[which].reshape(200, LANES))
            ev_s[which] = jnp.transpose(natural * (scales[which] * modulus[...]))
        for hop in range(1, n_event):
            event_copy(hop).start()

    index, older = 2, 3
    for moment in reversed(range(steps)):
        scaled = jnp.concatenate(
            [adjoint_gain * residuals[moment][comp] * rec_lane for comp in range(3)],
            axis=1,
        )
        injected = sum(dot(rows_lanes, part) for part in split3(scaled))
        for comp in range(3):
            force[comp] = injected[:, comp * LANES : (comp + 1) * LANES].reshape(
                5, 5, 8, LANES
            )

        def beside(moment=moment):
            add_kernels(moment, last_forward if moment == steps - 1 else None)
            if moment == steps - 1:
                put_out(last_forward, final_f_ref)
            if moment == 0:
                send_kernels()

        run_step(
            index,
            older,
            2 * steps - 1 - moment,
            astrain,
            lambda comp, a: force[comp, a],
            beside,
        )
        index, older = older, index

    put_out(index, final_a_ref)
    mine = pl.ds(pl.multiple_of(width * event, width), width)
    total = ev_s[:, mine]
    for hop in range(1, n_event):
        event_copy(hop).wait_recv()
        total = total + ev_r[hop - 1]
    out_ref[...] = total

    @pl.when(has_up)
    def _():
        up_copy(halo_s, halo_r, halo_slot).wait_send()
        for slot in range(2 * steps + 1):
            up_copy(up_s.at[slot], up_r.at[slot], slot).wait_send()

    @pl.when(has_down)
    def _():
        for slot in range(2 * steps + 1):
            down_copy(down_s.at[slot], down_r.at[slot], slot).wait_send()

    for hop in range(1, n_event):
        event_copy(hop).wait_send()


def on_device(
    n_mesh,
    n_event,
    forward_before,
    forward_now,
    adjoint_after,
    adjoint_now,
    mass_density,
    lame_lambda,
    lame_mu,
    source_element,
    source_offset,
    source_force,
    receiver_element,
    receiver_offset,
    receiver_data,
):
    assert forward_now.shape[1:] == (3, 8, 8, 128)
    assert lame_mu.shape == (125, 128)
    steps = source_force.shape[1]
    field = forward_now.shape
    vmem = pl.BlockSpec(memory_space=pltpu.VMEM)
    hbm = pl.BlockSpec(memory_space=pltpu.HBM)
    smem = pl.BlockSpec(memory_space=pltpu.SMEM)
    f32 = jnp.float32
    elem = (5, 5, 8, LANES)
    slots = 2 * steps + 1
    copied = (
        forward_now,
        forward_before,
        adjoint_now,
        adjoint_after,
        mass_density,
        lame_lambda,
        lame_mu,
        receiver_element,
        receiver_offset.transpose(2, 0, 1),
        receiver_data.transpose(1, 3, 0, 2),
    ) + constants()
    final_f, final_a, kernels = pl.pallas_call(
        functools.partial(kernel, n_mesh, n_event, steps),
        out_shape=(
            jax.ShapeDtypeStruct(field, f32),
            jax.ShapeDtypeStruct(field, f32),
            jax.ShapeDtypeStruct((2, LANES // n_event, 125), f32),
        ),
        in_specs=[hbm] * 15 + [smem] * 3,
        out_specs=(vmem, vmem, vmem),
        scratch_shapes=[pltpu.VMEM(value.shape, value.dtype) for value in copied]
        + [
            pltpu.SemaphoreType.DMA((len(copied),)),
            pltpu.VMEM((4, 3) + elem, f32),
            pltpu.VMEM((6,) + elem, f32),
            pltpu.VMEM((3,) + elem, f32),
            pltpu.VMEM((steps, 5, 6, 5, 8, LANES), f32),
            pltpu.VMEM((5, 6, 5, 8, LANES), f32),
            pltpu.VMEM((2,) + elem, f32),
            pltpu.VMEM(elem, f32),
            pltpu.VMEM(elem, f32),
            pltpu.VMEM(elem, f32),
            pltpu.VMEM((4, 3, 8, LANES), f32),
            pltpu.VMEM((4, 3, 8, LANES), f32),
            pltpu.VMEM((slots, 3, 2, 8, LANES), f32),
            pltpu.VMEM((slots, 3, 2, 8, LANES), f32),
            pltpu.VMEM((slots, 3, 2, 8, LANES), f32),
            pltpu.VMEM((slots, 3, 2, 8, LANES), f32),
            pltpu.VMEM((2, LANES, 125), f32),
            pltpu.VMEM((max(1, n_event - 1), 2, LANES // n_event, 125), f32),
            pltpu.SemaphoreType.DMA((slots + 1,)),
            pltpu.SemaphoreType.DMA((slots + 1,)),
            pltpu.SemaphoreType.DMA((slots,)),
            pltpu.SemaphoreType.DMA((slots,)),
            pltpu.SemaphoreType.DMA((max(1, n_event - 1),)),
            pltpu.SemaphoreType.DMA((max(1, n_event - 1),)),
        ],
        compiler_params=pltpu.CompilerParams(
            collective_id=0, has_side_effects=True, vmem_limit_bytes=60 * 1024 * 1024
        ),
    )(
        *copied,
        source_element,
        source_offset,
        source_force.transpose(1, 0, 2),
    )
    return (final_f, final_a, kernels.transpose(0, 2, 1))


def solution(mesh):
    return jax.shard_map(
        functools.partial(on_device, mesh.shape["mesh"], mesh.shape["event"]),
        mesh=mesh,
        in_specs=(
            P("event", None, "mesh", None, None),
            P("event", None, "mesh", None, None),
            P("event", None, "mesh", None, None),
            P("event", None, "mesh", None, None),
            P(None, "mesh"),
            P(None, "mesh"),
            P(None, "mesh"),
            P("event"),
            P("event", None),
            P("event", None, None),
            P("event", None),
            P("event", None, None),
            P("event", None, None, None),
        ),
        out_specs=(
            P("event", None, "mesh", None, None),
            P("event", None, "mesh", None, None),
            P(None, None, ("mesh", "event")),
        ),
        check_vma=False,
    )
```

```python
import functools
import math

import jax
import jax.numpy as jnp
import numpy as np
from jax import lax
from jax.experimental import pallas as pl
from jax.experimental.pallas import tpu as pltpu
from jax.sharding import PartitionSpec as P

time_step = 0.04
adjoint_gain = 25.0
LANES = 128


def numpy_tables():
    gll_points = np.array([-1.0, -math.sqrt(3.0 / 7.0), 0.0, math.sqrt(3.0 / 7.0), 1.0])
    legendre = (35.0 * gll_points**4 - 30.0 * gll_points**2 + 3.0) / 8.0
    deriv_table = np.zeros((5, 5))
    for row_q in range(5):
        for col_k in range(5):
            if row_q != col_k:
                deriv_table[row_q, col_k] = legendre[row_q] / (
                    legendre[col_k] * (gll_points[row_q] - gll_points[col_k])
                )
    deriv_table[0, 0] = -5.0
    deriv_table[4, 4] = 5.0
    gll_weights = np.array([0.1, 49.0 / 90.0, 32.0 / 45.0, 49.0 / 90.0, 0.1])
    return (deriv_table, gll_weights)


DERIV, WEIGHTS = numpy_tables()


def constants():
    spread = np.zeros((4, LANES, 4, 4, 32), np.float32)
    for j in range(4):
        for ex in range(32):
            for c in range(4):
                spread[j, 4 * ex + c, c, j, ex] = 1.0
    spread = spread.reshape(512, 512)
    rows = np.zeros((5, 5, 8, 125), np.float32)
    cube = np.zeros((5, 5, 8, LANES), np.float32)
    for a in range(5):
        for b in range(5):
            for c in range(5):
                rows[a, c, b, (a * 5 + b) * 5 + c] = 1.0
                cube[a, c, b, :] = WEIGHTS[a] * WEIGHTS[b] * WEIGHTS[c]
    rows = rows.reshape(200, 125)
    dy = np.zeros((2, 5, 8, LANES), np.float32)
    for k in range(5):
        for b in range(5):
            dy[0, k, b, :] = DERIV[b, k]
            dy[1, k, b, :] = DERIV[k, b]
    bf = jnp.bfloat16
    return (
        jnp.asarray(spread, bf),
        jnp.asarray(np.ascontiguousarray(spread.T), bf),
        jnp.asarray(rows, bf),
        jnp.asarray(cube),
        jnp.asarray(dy),
    )


def split3(value):
    high = value.astype(jnp.bfloat16)
    rest = value - high.astype(jnp.float32)
    middle = rest.astype(jnp.bfloat16)
    low = (rest - middle.astype(jnp.float32)).astype(jnp.bfloat16)
    return (high, middle, low)


def dot(left, right):
    return jnp.dot(left, right, preferred_element_type=jnp.float32)


def move_right(values, table):
    parts = split3(values)
    count = values.shape[0]
    stacked = jnp.concatenate(parts, axis=0)
    moved = dot(stacked, table)
    return moved[0:count] + moved[count : 2 * count] + moved[2 * count : 3 * count]


def move_left(table, values):
    high, middle, low = split3(values)
    return dot(table, high) + dot(table, middle) + dot(table, low)


def move_left_t(table, values):
    contract = (((0,), (0,)), ((), ()))
    return sum(
        lax.dot_general(table, part, contract, preferred_element_type=jnp.float32)
        for part in split3(values)
    )


def roll_lane(value, shift):
    return pltpu.roll(value, shift % LANES, value.ndim - 1)


def lane_iota(ndim):
    return lax.broadcasted_iota(jnp.int32, (1,) * (ndim - 1) + (LANES,), ndim - 1)


def sub_iota(ndim):
    return lax.broadcasted_iota(jnp.int32, (1,) * (ndim - 2) + (8, LANES), ndim - 2)


def pick(mask, first, second):
    return jnp.where(jnp.broadcast_to(mask, first.shape), first, second)


def from_left(value):
    at_edge = lane_iota(value.ndim) % 32 == 0
    return pick(at_edge, roll_lane(value, -31), roll_lane(value, 1))


def from_right(value):
    at_edge = lane_iota(value.ndim) % 32 == 31
    return pick(at_edge, roll_lane(value, 31), roll_lane(value, -1))


def roll_sub(value):
    return pltpu.roll(value, 4, value.ndim - 2)


def assemble_xy(value):
    first = value[:, 0:1] + from_left(value[:, 4:5])
    value = jnp.concatenate([first, value[:, 1:4], from_right(first)], axis=1)
    swapped = roll_sub(value)
    other = pick(
        lane_iota(4) % 64 < 32, roll_lane(swapped, -32), roll_lane(swapped, 32)
    )
    return value + pick(sub_iota(4) % 4 == 0, other, jnp.zeros_like(other))


def each(first, last, body):
    for a in range(first, last):
        body(a, 0)


def kernel(
    n_mesh,
    n_event,
    steps,
    now_hbm,
    before_hbm,
    adj_hbm,
    after_hbm,
    rho_hbm,
    lam_hbm,
    mu_hbm,
    rec_elem_hbm,
    rec_off_hbm,
    data_hbm,
    spread_hbm,
    gather_hbm,
    rows_hbm,
    cube_hbm,
    dy_hbm,
    elem_ref,
    off_ref,
    force_ref,
    final_f_ref,
    final_a_ref,
    out_ref,
    now_ref,
    before_ref,
    adj_ref,
    after_ref,
    rho_ref,
    lam_ref,
    mu_ref,
    rec_elem_ref,
    rec_off_ref,
    data_ref,
    spread_ref,
    gather_ref,
    rows_ref,
    cube_ref,
    dy_ref,
    s_in,
    fields,
    stress,
    force,
    strains,
    astrain,
    ksum,
    clam,
    cmu,
    minv,
    halo_s,
    halo_r,
    up_s,
    up_r,
    down_s,
    down_r,
    ev_s,
    ev_r,
    s_up,
    r_up,
    s_down,
    r_down,
    s_ev,
    r_ev,
):
    me = lax.axis_index("mesh")
    event = lax.axis_index("event")
    has_up = me > 0
    has_down = me < n_mesh - 1

    loads = []
    pairs = (
        (now_hbm, now_ref),
        (before_hbm, before_ref),
        (adj_hbm, adj_ref),
        (after_hbm, after_ref),
        (rows_hbm, rows_ref),
        (lam_hbm, lam_ref),
        (mu_hbm, mu_ref),
        (rho_hbm, rho_ref),
        (cube_hbm, cube_ref),
        (spread_hbm, spread_ref),
        (dy_hbm, dy_ref),
        (rec_elem_hbm, rec_elem_ref),
        (rec_off_hbm, rec_off_ref),
        (data_hbm, data_ref),
        (gather_hbm, gather_ref),
    )
    for place, (source, target) in enumerate(pairs):
        load_copy = pltpu.make_async_copy(source, target, s_in.at[place])
        load_copy.start()
        loads.append(load_copy)

    barrier = pltpu.get_barrier_semaphore()

    @pl.when(has_up)
    def _():
        pl.semaphore_signal(barrier, inc=1, device_id={"mesh": me - 1})

    @pl.when(has_down)
    def _():
        pl.semaphore_signal(barrier, inc=1, device_id={"mesh": me + 1})

    for hop in range(1, n_event):
        pl.semaphore_signal(
            barrier, inc=1, device_id={"event": lax.rem(event + hop, n_event)}
        )

    inputs = (now_ref, before_ref, adj_ref, after_ref)
    for place in range(4):
        loads[place].wait()
    for index, ref in enumerate(inputs):
        halo_s[index] = ref[0, :, 0]

    pl.semaphore_wait(
        barrier,
        jnp.where(has_up, 1, 0) + jnp.where(has_down, 1, 0) + (n_event - 1),
    )

    def up_copy(source, target, slot):
        return pltpu.make_async_remote_copy(
            src_ref=source, dst_ref=target, send_sem=s_up.at[slot],
            recv_sem=r_up.at[slot], device_id={"mesh": me - 1},
        )

    def down_copy(source, target, slot):
        return pltpu.make_async_remote_copy(
            src_ref=source, dst_ref=target, send_sem=s_down.at[slot],
            recv_sem=r_down.at[slot], device_id={"mesh": me + 1},
        )

    halo_slot = steps * 2 + 1

    @pl.when(has_up)
    def _():
        up_copy(halo_s, halo_r, halo_slot).start()

    @pl.when(jnp.logical_not(has_down))
    def _():
        halo_r[...] = jnp.zeros_like(halo_r)
        up_r[...] = jnp.zeros_like(up_r)

    @pl.when(jnp.logical_not(has_up))
    def _():
        down_r[...] = jnp.zeros_like(down_r)

    low_half = lane_iota(4) < 64

    def send_faces(top, bottom, slot):
        count = top.shape[0]
        for pair in range(2):
            c = 2 * pair
            up_s[slot, 0:count, pair] = pick(
                low_half, top[:, c : c + 1], roll_lane(top[:, c + 1 : c + 2], 64)
            )[:, 0]
            down_s[slot, 0:count, pair] = pick(
                low_half, roll_lane(bottom[:, c : c + 1], 64), bottom[:, c + 1 : c + 2]
            )[:, 0]

        @pl.when(has_up)
        def _():
            up_copy(up_s.at[slot], up_r.at[slot], slot).start()

        @pl.when(has_down)
        def _():
            down_copy(down_s.at[slot], down_r.at[slot], slot).start()

    def finish_faces(top, bottom, slot):
        count = top.shape[0]

        @pl.when(has_down)
        def _():
            up_copy(up_s.at[slot], up_r.at[slot], slot).wait_recv()

        @pl.when(has_up)
        def _():
            down_copy(down_s.at[slot], down_r.at[slot], slot).wait_recv()

        below = []
        above = []
        for pair in range(2):
            packed = up_r[slot, 0:count, pair : pair + 1]
            below += [roll_lane(packed, 64), packed]
            packed = down_r[slot, 0:count, pair : pair + 1]
            above += [packed, roll_lane(packed, 64)]
        below.append(from_right(below[0]))
        above.append(from_right(above[0]))
        below = jnp.concatenate(below, axis=1)
        above = jnp.concatenate(above, axis=1)
        new_top = top + pick(low_half, above, roll_lane(bottom, 64))
        new_bottom = bottom + pick(low_half, roll_lane(top, 64), below)
        return (new_top, new_bottom)

    for place in range(4, 9):
        loads[place].wait()
    materials = jnp.concatenate([lam_ref[...], mu_ref[...], rho_ref[...]], axis=1)
    moved = move_left(rows_ref[...], materials)
    cube = cube_ref[...]
    clam[...] = moved[:, 0:128].reshape(5, 5, 8, LANES) * cube
    cmu[...] = moved[:, 128:256].reshape(5, 5, 8, LANES) * cube
    mass = moved[:, 256:384].reshape(5, 5, 8, LANES) * cube
    mass = [assemble_xy(mass[a : a + 1]) for a in range(5)]
    mass_slot = steps * 2
    send_faces(mass[0], mass[4], mass_slot)

    for place in range(9, 14):
        loads[place].wait()
    nrec = rec_elem_ref.shape[1]
    elem = rec_elem_ref[...] - LANES * me
    lane_t = lax.broadcasted_iota(jnp.int32, (LANES, nrec), 0) == elem
    lane_t = jnp.where(lane_t, 1.0, 0.0).astype(jnp.bfloat16)
    eye = jnp.where(
        lax.broadcasted_iota(jnp.int32, (nrec, nrec), 0)
        == lax.broadcasted_iota(jnp.int32, (nrec, nrec), 1),
        1.0,
        0.0,
    ).astype(jnp.bfloat16)
    turned = (((1,), (1,)), ((), ()))

    def turn(part):
        return lax.dot_general(eye, part, turned, preferred_element_type=jnp.float32)

    rec_lane = turn(lane_t)
    row = rec_off_ref[0] * 40 + rec_off_ref[2] * 8 + rec_off_ref[1]
    rows_lanes = lax.broadcasted_iota(jnp.int32, (200, nrec), 0) == row
    rows_lanes = jnp.where(rows_lanes, 1.0, 0.0).astype(jnp.bfloat16)
    rec_rows = turn(rows_lanes).astype(jnp.bfloat16)
    observed = jnp.concatenate(
        [data_ref[n, comp] for n in range(steps) for comp in range(3)], axis=0
    )
    observed = sum(turn(part) for part in split3(observed))
    src_row = off_ref[0, 0] * 40 + off_ref[0, 2] * 8 + off_ref[0, 1]
    src_lane = elem_ref[0] - LANES * me

    @pl.when(has_down)
    def _():
        up_copy(halo_s, halo_r, halo_slot).wait_recv()

    def bring_in(index):
        ref = inputs[index]
        layer0 = ref[0, :, 0:5]
        layer1 = jnp.concatenate([ref[0, :, 4:8], halo_r[index][:, None]], axis=1)
        parts = []
        for layer in (layer0, layer1):
            for shifted in (layer, roll_sub(layer)):
                parts.append(shifted.reshape(120, LANES))
        moved = move_right(jnp.concatenate(parts, axis=1), spread_ref[...])
        for c in range(4):
            fields[index, :, :, c] = moved[:, c * LANES : (c + 1) * LANES].reshape(
                3, 5, 8, LANES
            )
        fields[index, :, :, 4] = from_right(
            moved[:, 0:LANES].reshape(3, 5, 8, LANES)
        )

    def finish_mass():
        top, bottom = finish_faces(mass[0], mass[4], mass_slot)
        real_row = sub_iota(4) < 5
        for a in range(5):
            plane = top if a == 0 else (bottom if a == 4 else mass[a])
            keep = real_row
            if a == 4:
                keep = keep & ((lane_iota(4) < 64) | has_down)
            keep = jnp.broadcast_to(keep, plane.shape)
            safe = jnp.where(keep, plane, 1.0)
            minv[a] = jnp.where(keep, time_step**2 / safe, 0.0)[0]

    bring_in(0)

    def strain_at(index, a):
        plane = fields[index, :, a]
        gx = []
        for c in range(5):
            total = None
            for k in range(5):
                if DERIV[c, k] == 0.0:
                    continue
                term = float(DERIV[c, k]) * plane[:, k]
                total = term if total is None else total + term
            gx.append(total[:, None])
        gx = jnp.concatenate(gx, axis=1)
        gy = None
        gz = None
        for k in range(5):
            row_k = jnp.broadcast_to(plane[:, :, k : k + 1], plane.shape)
            term = dy_ref[0, k] * row_k
            gy = term if gy is None else gy + term
            if DERIV[a, k] != 0.0:
                term = float(DERIV[a, k]) * fields[index, :, k]
                gz = term if gz is None else gz + term
        return (
            gx[0],
            gy[1],
            gz[2],
            gy[0] + gx[1],
            gz[0] + gx[2],
            gz[1] + gy[2],
        )

    def add_kernels(moment, last_index):
        def body(a, carry):
            strain = [astrain[a, i] for i in range(6)]
            if last_index is None:
                other = [strains[moment, a, i] for i in range(6)]
            else:
                other = strain_at(last_index, a)
            div_a = strain[0] + strain[1] + strain[2]
            div_f = other[0] + other[1] + other[2]
            diag = strain[0] * other[0] + strain[1] * other[1] + strain[2] * other[2]
            shear = strain[3] * other[3] + strain[4] * other[4] + strain[5] * other[5]
            lam_part = div_a * div_f
            mu_part = diag + 0.5 * shear
            if last_index is not None:
                ksum[0, a] = lam_part
                ksum[1, a] = mu_part
            else:
                ksum[0, a] = ksum[0, a] + lam_part
                ksum[1, a] = ksum[1, a] + mu_part
            return carry

        each(0, 5, body)

    def run_step(index, older, slot, keep_strain, load, beside):
        def stress_body(a, carry):
            strain = strain_at(index, a)
            lam_div = clam[a] * (strain[0] + strain[1] + strain[2])
            mu_a = cmu[a]
            mu_two = mu_a + mu_a
            for i in range(3):
                stress[i, a] = lam_div + mu_two * strain[i]
                stress[3 + i, a] = mu_a * strain[3 + i]
            if keep_strain is not None:
                for i in range(6):
                    keep_strain[a, i] = strain[i]
            return carry

        each(0, 5, stress_body)

        def force_body(a, carry):
            along = ((0, 3, 4), (3, 1, 5), (4, 5, 2))
            for comp in range(3):
                sx = stress[along[comp][0], a]
                sy = stress[along[comp][1], a]
                pieces = []
                for c in range(5):
                    total = None
                    for q in range(5):
                        if DERIV[q, c] == 0.0:
                            continue
                        term = float(DERIV[q, c]) * sx[q]
                        total = term if total is None else total + term
                    pieces.append(total[None])
                total = jnp.concatenate(pieces, axis=0)
                for q in range(5):
                    row_q = jnp.broadcast_to(sy[:, q : q + 1], sy.shape)
                    total = total + dy_ref[1, q] * row_q
                    if DERIV[q, a] != 0.0:
                        total = total + float(DERIV[q, a]) * stress[along[comp][2], q]
                force[comp, a] = total - load(comp, a)
            force[:, a] = assemble_xy(force[:, a])
            return carry

        force_body(0, 0)
        force_body(4, 0)
        send_faces(force[:, 0], force[:, 4], slot)
        beside()

        def inner(a, carry):
            fields[older, :, a] = (
                2.0 * fields[index, :, a] - fields[older, :, a]
            ) - minv[a] * force[:, a]
            return carry

        each(1, 4, force_body)
        each(1, 4, inner)
        top, bottom = finish_faces(force[:, 0], force[:, 4], slot)
        for a, plane in ((0, top), (4, bottom)):
            fields[older, :, a] = (
                2.0 * fields[index, :, a] - fields[older, :, a]
            ) - minv[a] * plane

    def record(index, moment):
        values = jnp.concatenate(
            [fields[index, comp].reshape(200, LANES) for comp in range(3)], axis=1
        )
        at_rows = move_left(rec_rows, values)
        found = []
        for comp in range(3):
            seen = at_rows[:, comp * LANES : (comp + 1) * LANES] * rec_lane
            found.append(
                jnp.sum(seen, axis=1, keepdims=True)
                - observed[:, 3 * moment + comp : 3 * moment + comp + 1]
            )
        return found

    residuals = []

    index, older = 0, 1
    for moment in range(steps):
        def source_load(comp, a, moment=moment):
            here = (lax.broadcasted_iota(jnp.int32, (5, 8, LANES), 0) * 8
                    + lax.broadcasted_iota(jnp.int32, (5, 8, LANES), 1)
                    + a * 40) == src_row
            there = lax.broadcasted_iota(jnp.int32, (5, 8, LANES), 2) == src_lane
            return jnp.where(here & there, force_ref[moment, 0, comp], 0.0)

        def beside(moment=moment, index=index):
            if moment == 0:
                bring_in(1)
                finish_mass()
            else:
                residuals.append(record(index, moment - 1))
            if moment == min(1, steps - 1):
                bring_in(2)
            if moment == steps - 1:
                bring_in(3)

        run_step(
            index,
            older,
            moment,
            strains.at[moment - 1] if moment > 0 else None,
            source_load,
            beside,
        )
        index, older = older, index
    residuals.append(record(index, steps - 1))
    last_forward = index
    loads[14].wait()

    def put_out(index, ref):
        sides = [fields[index, :, 0:4, c].reshape(96, LANES) for c in range(4)]
        moved = move_right(jnp.concatenate(sides, axis=1), gather_ref[...])
        for ez in range(2):
            first = moved[:, 2 * ez * LANES : (2 * ez + 1) * LANES]
            second = moved[:, (2 * ez + 1) * LANES : (2 * ez + 2) * LANES]
            first = first.reshape(3, 4, 8, LANES)
            second = roll_sub(second.reshape(3, 4, 8, LANES))
            ref[0, :, 4 * ez : 4 * ez + 4] = pick(sub_iota(4) < 4, first, second)

    width = LANES // n_event

    def event_copy(hop):
        target = lax.rem(event + hop, n_event)
        return pltpu.make_async_remote_copy(
            src_ref=ev_s.at[:, pl.ds(pl.multiple_of(width * target, width), width)],
            dst_ref=ev_r.at[hop - 1],
            send_sem=s_ev.at[hop - 1],
            recv_sem=r_ev.at[hop - 1],
            device_id={"event": target},
        )

    def send_kernels():
        scales = (-time_step, -2.0 * time_step)
        for which, modulus in enumerate((lam_ref, mu_ref)):
            natural = move_left_t(rows_ref[...], ksum[which].reshape(200, LANES))
            ev_s[which] = jnp.transpose(natural * (scales[which] * modulus[...]))
        for hop in range(1, n_event):
            event_copy(hop).start()

    index, older = 2, 3
    for moment in reversed(range(steps)):
        scaled = jnp.concatenate(
            [adjoint_gain * residuals[moment][comp] * rec_lane for comp in range(3)],
            axis=1,
        )
        injected = sum(dot(rows_lanes, part) for part in split3(scaled))
        for comp in range(3):
            force[comp] = injected[:, comp * LANES : (comp + 1) * LANES].reshape(
                5, 5, 8, LANES
            )

        def beside(moment=moment):
            add_kernels(moment, last_forward if moment == steps - 1 else None)
            if moment == max(steps - 2, 0):
                put_out(last_forward, final_f_ref)
            if moment == 0:
                send_kernels()

        run_step(
            index,
            older,
            2 * steps - 1 - moment,
            astrain,
            lambda comp, a: force[comp, a],
            beside,
        )
        index, older = older, index

    put_out(index, final_a_ref)
    mine = pl.ds(pl.multiple_of(width * event, width), width)
    total = ev_s[:, mine]
    for hop in range(1, n_event):
        event_copy(hop).wait_recv()
        total = total + ev_r[hop - 1]
    out_ref[...] = total

    @pl.when(has_up)
    def _():
        up_copy(halo_s, halo_r, halo_slot).wait_send()
        for slot in range(2 * steps + 1):
            up_copy(up_s.at[slot], up_r.at[slot], slot).wait_send()

    @pl.when(has_down)
    def _():
        for slot in range(2 * steps + 1):
            down_copy(down_s.at[slot], down_r.at[slot], slot).wait_send()

    for hop in range(1, n_event):
        event_copy(hop).wait_send()


def on_device(
    n_mesh,
    n_event,
    forward_before,
    forward_now,
    adjoint_after,
    adjoint_now,
    mass_density,
    lame_lambda,
    lame_mu,
    source_element,
    source_offset,
    source_force,
    receiver_element,
    receiver_offset,
    receiver_data,
):
    assert forward_now.shape[1:] == (3, 8, 8, 128)
    assert lame_mu.shape == (125, 128)
    steps = source_force.shape[1]
    field = forward_now.shape
    vmem = pl.BlockSpec(memory_space=pltpu.VMEM)
    hbm = pl.BlockSpec(memory_space=pltpu.HBM)
    smem = pl.BlockSpec(memory_space=pltpu.SMEM)
    f32 = jnp.float32
    elem = (5, 5, 8, LANES)
    slots = 2 * steps + 1
    copied = (
        forward_now,
        forward_before,
        adjoint_now,
        adjoint_after,
        mass_density,
        lame_lambda,
        lame_mu,
        receiver_element,
        receiver_offset.transpose(2, 0, 1),
        receiver_data.transpose(1, 3, 0, 2),
    ) + constants()
    final_f, final_a, kernels = pl.pallas_call(
        functools.partial(kernel, n_mesh, n_event, steps),
        out_shape=(
            jax.ShapeDtypeStruct(field, f32),
            jax.ShapeDtypeStruct(field, f32),
            jax.ShapeDtypeStruct((2, LANES // n_event, 125), f32),
        ),
        in_specs=[hbm] * 15 + [smem] * 3,
        out_specs=(vmem, vmem, vmem),
        scratch_shapes=[pltpu.VMEM(value.shape, value.dtype) for value in copied]
        + [
            pltpu.SemaphoreType.DMA((len(copied),)),
            pltpu.VMEM((4, 3) + elem, f32),
            pltpu.VMEM((6,) + elem, f32),
            pltpu.VMEM((3,) + elem, f32),
            pltpu.VMEM((steps, 5, 6, 5, 8, LANES), f32),
            pltpu.VMEM((5, 6, 5, 8, LANES), f32),
            pltpu.VMEM((2,) + elem, f32),
            pltpu.VMEM(elem, f32),
            pltpu.VMEM(elem, f32),
            pltpu.VMEM(elem, f32),
            pltpu.VMEM((4, 3, 8, LANES), f32),
            pltpu.VMEM((4, 3, 8, LANES), f32),
            pltpu.VMEM((slots, 3, 2, 8, LANES), f32),
            pltpu.VMEM((slots, 3, 2, 8, LANES), f32),
            pltpu.VMEM((slots, 3, 2, 8, LANES), f32),
            pltpu.VMEM((slots, 3, 2, 8, LANES), f32),
            pltpu.VMEM((2, LANES, 125), f32),
            pltpu.VMEM((max(1, n_event - 1), 2, LANES // n_event, 125), f32),
            pltpu.SemaphoreType.DMA((slots + 1,)),
            pltpu.SemaphoreType.DMA((slots + 1,)),
            pltpu.SemaphoreType.DMA((slots,)),
            pltpu.SemaphoreType.DMA((slots,)),
            pltpu.SemaphoreType.DMA((max(1, n_event - 1),)),
            pltpu.SemaphoreType.DMA((max(1, n_event - 1),)),
        ],
        compiler_params=pltpu.CompilerParams(
            collective_id=0, has_side_effects=True, vmem_limit_bytes=60 * 1024 * 1024
        ),
    )(
        *copied,
        source_element,
        source_offset,
        source_force.transpose(1, 0, 2),
    )
    return (final_f, final_a, kernels.transpose(0, 2, 1))


def solution(mesh):
    return jax.shard_map(
        functools.partial(on_device, mesh.shape["mesh"], mesh.shape["event"]),
        mesh=mesh,
        in_specs=(
            P("event", None, "mesh", None, None),
            P("event", None, "mesh", None, None),
            P("event", None, "mesh", None, None),
            P("event", None, "mesh", None, None),
            P(None, "mesh"),
            P(None, "mesh"),
            P(None, "mesh"),
            P("event"),
            P("event", None),
            P("event", None, None),
            P("event", None),
            P("event", None, None),
            P("event", None, None, None),
        ),
        out_specs=(
            P("event", None, "mesh", None, None),
            P("event", None, "mesh", None, None),
            P(None, None, ("mesh", "event")),
        ),
        check_vma=False,
    )
```
